32 devices in a mesh: seq: 8 (over y, x, core), dp: 4 (over z).
Axes of the slice: x: 2, y: 2, z: 4, core: 2. Of those that a mesh axis runs over, the one named last changes fastest.
Arguments:
- queries: bfloat16 [4096, 512], P('seq', 'dp'), may hold values from -40 to 40
- keys: bfloat16 [4096, 512], P('seq', 'dp'), may hold values from -40 to 40
- values: bfloat16 [4096, 512], P('seq', 'dp'), may hold values from -6 to 6
- cross_queries: bfloat16 [4096, 512], P('seq', 'dp'), may hold values from -90 to 90
- encoded: bfloat16 [64, 128, 896], P('dp'), may hold values from -6 to 6
- cross_kv_weight: bfloat16 [896, 2, 512], P(None, None, 'dp'), may hold values from -0.1875 to 0.1875
- owners: int32 [64, 2], P('seq'), may hold values from 0 to 3, all different within a row; in each aligned block of 8 rows (0 to 7, 8 to 15, ...) at most 8 rows name the same one
- tile_rows: int32 [64, 2], P('seq'), may hold values from 0 to 15
Outputs:
- attended: bfloat16 [4096, 512], P('seq', 'dp')
- crossed: bfloat16 [4096, 512], P('seq', 'dp')
The draws below stay inside these ranges and needn't reach their ends.
Inputs may be any that keep to these rules, and one draw needn't show every extreme that they name: `owners`: the 2 entries of a row differ; in each aligned block of 8 rows (the spans of one seq index) no owner is named by more than 8 rows, a bound that some block reaches.
All inputs are finite; a program needn't handle non-finite values.
Results may differ from the reference program's by a relative error of at most 0.0083.
Values may be sent and summed in bfloat16 or wider, within the bound.
A program may use at most 128 MiB of HBM per device.

```python
import math
import jax
import jax.numpy as jnp
import numpy as np
from jax import lax

CL = 64
NB = 2
RL = 128
HS = 128
ENC = 896
POOL_DEV = 16
HEADS = 4
LEN = 4096
SPANS = 64
SPANS_DEV = 8
POOL = 64
CAP = 8
N_DP = 4


def paired_draw(key):
    base = jax.random.fold_in(key, 11)
    key_query, key_key = jax.random.split(base, 2)
    shape = (LEN, HEADS * HS)
    query_part = jnp.clip(1.7 * jax.random.normal(key_query, shape, jnp.float32), -6.8, 6.8)
    key_part = jnp.clip(1.7 * jax.random.normal(key_key, shape, jnp.float32), -6.8, 6.8)
    return (query_part, key_part)


def draw_queries(key, part):
    return paired_draw(key)[0].astype(jnp.bfloat16)


def draw_keys(key, part):
    return paired_draw(key)[1].astype(jnp.bfloat16)


def draw_cross_queries(key, part):
    base = jax.random.fold_in(key, 23)
    shape = (LEN, HEADS * HS)
    sample = jnp.clip(1.7 * jax.random.normal(base, shape, jnp.float32), -6.8, 6.8)
    return sample.astype(jnp.bfloat16)


def set_ends(entries, rng, least, largest):
    longest = entries.shape.index(max(entries.shape))
    spots = []
    for shift in (0, 1):
        where = [jax.random.randint(jax.random.fold_in(rng, axis), (), 0, length) for axis, length in enumerate(entries.shape)]
        where[longest] = (where[longest] + shift) % entries.shape[longest]
        spots.append(tuple(where))
    return entries.at[spots[0]].set(least).at[spots[1]].set(largest)


def steps_of(key, extent, cuts, smallest, top_value):
    factor_of, own = 1.0, jax.random.fold_in(key, 6)
    for axis_at, shards_of in cuts:
        steps = jnp.exp(jax.random.uniform(jax.random.fold_in(own, axis_at), (shards_of,), jnp.float32, smallest / len(cuts), top_value / len(cuts)))
        factor_of = factor_of * jnp.repeat(steps, extent[axis_at] // shards_of).reshape([-1 if axis == axis_at else 1 for axis in range(len(extent))])
    return factor_of


def shared_out(rng, own, number, rows, count, top, reach, slope):
    order = jax.random.permutation(rng, count)
    crowded, usual = portions_of(count, rows * top, reach, slope, True), portions_of(count, rows * top, reach, slope, False)
    places = jnp.arange(count)

    def named(tallies, offset_by):
        used = int((tallies > 0).sum())
        fixed = max(1, used // 4)
        shifted = fixed + (places - fixed + offset_by * (used - fixed)) % max(1, count - fixed)
        return jnp.zeros((count,), jnp.int32).at[order[jnp.where(places < fixed, places, shifted)]].set(jnp.asarray(tallies, jnp.int32))

    tallies = jnp.where(number % 4 == 0, named(crowded, number // 4), named(usual, number - number // 4 - 1))
    mixed = jax.random.permutation(jax.random.fold_in(own, 3), count)
    donor, sink = mixed[0:count // 2 * 2:2], mixed[1:count // 2 * 2:2]
    room = jnp.minimum(tallies[donor] - 1, reach - tallies[sink]) // 2
    room = jnp.where((donor == order[0]) | (sink == order[0]) | (tallies[sink] == 0), 0, jnp.maximum(room, 0))
    shifted = jax.random.randint(jax.random.fold_in(own, 4), (count // 2,), 0, 1 << 20) % (room + 1)
    tallies = tallies.at[donor].add(-shifted).at[sink].add(shifted)
    items = jnp.searchsorted(jnp.cumsum(tallies), jnp.arange(rows * top), side="right").astype(jnp.int32)
    grid = items.reshape(top, rows).T
    grid = grid[jax.random.permutation(jax.random.fold_in(own, 1), rows)]
    offset_by = jax.random.randint(jax.random.fold_in(own, 2), (rows, 1), 0, top)
    return jnp.take_along_axis(grid, (jnp.arange(top)[None, :] + offset_by) % top, axis=1)


def portions_of(amount, total, reach, lean, full):
    weights = [(1 << 20) // math.isqrt(rank ** lean) + 1 for rank in range(1, amount + 1)]
    largest = reach if full else min(reach, max(-(-total // amount), total * weights[0] // sum(weights)))
    least = 1 if total - largest >= amount - 1 else 0
    counts, surplus = [largest] + [least] * (amount - 1), total - largest - least * (amount - 1)
    while surplus > 0:
        free = [i for i in range(1, amount) if counts[i] < largest] or [i for i in range(1, amount) if counts[i] < reach]
        whole, left = sum([weights[i] for i in free]), surplus
        for i in free:
            more = min(reach - counts[i], max(1, left * weights[i] // whole), surplus)
            counts[i] = counts[i] + more
            surplus = surplus - more
    return np.array(counts)


def noise(key, dims, deviation, reach, pieces=(), held_as=jnp.bfloat16):
    drawn = jax.random.normal(key, dims, jnp.float32) * deviation
    if len(pieces) > 0:
        drawn = steps_of(key, dims, pieces, -0.22, 0.18) * drawn
    return jnp.clip(drawn, min=-reach, max=reach).astype(held_as)


def setup_inputs(seed: int = 0) -> dict:
    key_of = jax.random.split(jax.random.key(seed), 9)
    queries = draw_queries(jax.random.fold_in(key_of[8], 71), 0)
    keys = draw_keys(jax.random.fold_in(key_of[8], 71), 0)
    values = noise(key_of[2], (LEN, HEADS * HS), 1.0, 6.0, ((0, 8), (1, 4)))
    cross_queries = draw_cross_queries(jax.random.fold_in(key_of[8], 71), 0)
    encoded = noise(key_of[4], (POOL, RL, ENC), 1.0, 6.0, ((0, 4),))
    cross_kv_weight = noise(key_of[5], (ENC, 2, HEADS * HS), ENC ** -0.5, 0.1875, ((2, 4),))
    owners_keys = jax.random.split(jax.random.fold_in(key_of[6], 1), SPANS // SPANS_DEV)
    owners_turns = jax.random.permutation(jax.random.fold_in(key_of[6], 3), SPANS // SPANS_DEV)
    owners = jax.vmap(lambda own, number: shared_out(jax.random.fold_in(key_of[6], 2), own, number, SPANS_DEV, N_DP, NB, CAP, 2))(owners_keys, owners_turns).reshape((SPANS, NB))
    tile_rows = set_ends(jax.random.randint(key_of[7], (SPANS, NB), 0, POOL_DEV), jax.random.fold_in(key_of[7], 1), 0, POOL_DEV - 1).astype(jnp.int32)
    return {"queries": queries, "keys": keys, "values": values, "cross_queries": cross_queries, "encoded": encoded, "cross_kv_weight": cross_kv_weight, "owners": owners, "tile_rows": tile_rows}


def self_head(head_arrays):
    query_head, key_head, value_head = head_arrays
    block_rows = math.gcd(LEN, 512)
    query_blocks = query_head.reshape(LEN // block_rows, block_rows, HS)
    starts = jnp.arange(LEN // block_rows, dtype=jnp.int32) * block_rows
    inv_root = 1.0 / math.sqrt(HS)
    key_positions = jnp.arange(LEN, dtype=jnp.int32)

    def one_block(item):
        query_block, first_row = item
        scores = jnp.dot(query_block, key_head.T, preferred_element_type=jnp.float32) * inv_root
        positions = first_row + jnp.arange(block_rows, dtype=jnp.int32)
        allowed = key_positions[None, :] <= positions[:, None]
        scores = jnp.where(allowed, scores, jnp.float32(-1e+30))
        row_max = lax.optimization_barrier(jnp.max(scores, axis=1, keepdims=True))
        expo = jnp.where(allowed, jnp.exp(scores - row_max), jnp.float32(0.0))
        total = lax.optimization_barrier(jnp.sum(expo, axis=1, keepdims=True))
        weights = expo.astype(jnp.bfloat16)
        summed = jnp.dot(weights, value_head, preferred_element_type=jnp.float32)
        return (summed / total).astype(jnp.bfloat16)
    return lax.map(one_block, (query_blocks, starts)).reshape(LEN, HS)

def reference(queries, keys, values, cross_queries, encoded, cross_kv_weight, owners, tile_rows):
    width = HEADS * HS
    inv_root = 1.0 / math.sqrt(HS)
    query_heads = queries.reshape(LEN, HEADS, HS).transpose(1, 0, 2)
    key_heads = keys.reshape(LEN, HEADS, HS).transpose(1, 0, 2)
    value_heads = values.reshape(LEN, HEADS, HS).transpose(1, 0, 2)
    head_outs = lax.map(self_head, (query_heads, key_heads, value_heads))
    attended = head_outs.transpose(1, 0, 2).reshape(LEN, width)
    tile_index = (owners * POOL_DEV + tile_rows).astype(jnp.int32)
    padded = jnp.concatenate([cross_queries[CL - 1:], jnp.zeros((CL - 1, width), jnp.bfloat16)], axis=0)
    span_queries = padded.reshape(SPANS, CL, HEADS, HS)
    flat_weight = cross_kv_weight.reshape(ENC, 2 * width)

    def one_span(item):
        query_block, indices = item
        tiles = jnp.take(encoded, indices, axis=0).reshape(NB * RL, ENC)
        projected = jnp.dot(tiles, flat_weight, preferred_element_type=jnp.float32).astype(jnp.bfloat16)
        projected = projected.reshape(NB * RL, 2, HEADS, HS)
        cross_keys = projected[:, 0]
        cross_values = projected[:, 1]
        scores = jnp.einsum('qhd,khd->hqk', query_block.astype(jnp.float32), cross_keys.astype(jnp.float32)) * inv_root
        row_max = lax.optimization_barrier(jnp.max(scores, axis=2, keepdims=True))
        expo = jnp.exp(scores - row_max)
        total = lax.optimization_barrier(jnp.sum(expo, axis=2))
        weights = expo.astype(jnp.bfloat16)
        summed = jnp.einsum('hqk,khd->qhd', weights.astype(jnp.float32), cross_values.astype(jnp.float32))
        result = summed / jnp.transpose(total)[:, :, None]
        return result.reshape(CL, width).astype(jnp.bfloat16)
    span_outs = lax.map(one_span, (span_queries, tile_index)).reshape(LEN, width)
    crossed = jnp.concatenate([jnp.zeros((CL - 1, width), jnp.bfloat16), span_outs[:LEN - CL + 1]], axis=0)
    return (attended, crossed)
```

```python
import functools
import math

import jax
import jax.numpy as jnp
from jax import lax
from jax.experimental import pallas as pl
from jax.experimental.pallas import tpu as pltpu
from jax.sharding import PartitionSpec as P

HS = 128
NEG = -1e30
MESH = pl.DeviceIdType.MESH


def kernel(
    S, D, tile_len, inv_root,
    ids, q, key, val, cq, enc, w,
    att, crs,
    encv, wall, pbuf, pool, kall, vall, m_ref, l_ref, acc_ref,
    enc_sem, send_w, recv_w, send_p, recv_p, send_x, recv_x, send_s, recv_s,
    send_k, recv_k, send_ks, recv_ks,
):
    C = 2
    G = S // C
    s = lax.axis_index("seq")
    d = lax.axis_index("dp")
    g = s // C
    k = s % C
    sib = g * C + (1 - k)
    T = q.shape[0]
    rows_g = encv.shape[0]
    spans = ids.shape[0]
    span_len = cq.shape[0] // spans

    enc_copy = pltpu.make_async_copy(
        enc.at[pl.ds(pl.multiple_of(g * rows_g, rows_g), rows_g)], encv, enc_sem
    )
    enc_copy.start()

    bar = pltpu.get_barrier_semaphore()

    @pl.loop(1, G)
    def _(o):
        pl.semaphore_signal(bar, 1, device_id={"seq": ((g + o) % G) * C + k}, device_id_type=MESH)

    pl.semaphore_signal(bar, 1, device_id={"seq": sib}, device_id_type=MESH)

    @pl.loop(1, D)
    def _(o):
        pl.semaphore_signal(bar, 1, device_id={"dp": (d + o) % D}, device_id_type=MESH)

    pl.semaphore_wait(bar, G - 1 + 1 + D - 1)

    unit = pool.shape[2]
    units_g = rows_g // unit
    units_tile = tile_len // unit

    def block(plane, group):
        return pl.ds((plane * G + group) * units_g, units_g)

    def w_own(side):
        return pltpu.make_async_remote_copy(
            w.at[k], wall.at[d], send_w.at[side, d], recv_w.at[d],
            device_id={"dp": d + (1 if side else -1)}, device_id_type=MESH)

    def w_pass(src, side):
        return pltpu.make_async_remote_copy(
            wall.at[src], wall.at[src], send_w.at[side, src], recv_w.at[src],
            device_id={"dp": d + (1 if side else -1)}, device_id_type=MESH)

    def p_copy(to, src):
        return pltpu.make_async_remote_copy(
            pbuf.at[to], pool.at[k, block(src, g)], send_p.at[to], recv_p.at[src],
            device_id={"dp": to}, device_id_type=MESH)

    def x_copy(plane, src, to):
        return pltpu.make_async_remote_copy(
            pool.at[k, block(plane, src)], pool.at[k, block(plane, src)],
            send_x.at[plane, to], recv_x.at[plane, src],
            device_id={"seq": to * C + k}, device_id_type=MESH)

    def s_copy(plane, src, kv):
        return pltpu.make_async_remote_copy(
            pool.at[kv, block(plane, src)], pool.at[kv, block(plane, src)],
            send_s.at[plane, src], recv_s.at[plane, src],
            device_id={"seq": sib}, device_id_type=MESH)

    parts = ((0, key, kall), (1, val, vall))

    def kv_copy(i, ref, land, src, to):
        return pltpu.make_async_remote_copy(
            ref, land.at[src * C + k], send_k.at[i, to], recv_k.at[i, src],
            device_id={"seq": to * C + k}, device_id_type=MESH)

    def kv_sib(i, src_ref, land, src, kk):
        return pltpu.make_async_remote_copy(
            src_ref, land.at[src * C + kk], send_ks.at[i, src], recv_ks.at[i, src],
            device_id={"seq": sib}, device_id_type=MESH)

    for side in (0, 1):
        @pl.when((d + 1 < D) if side else (d > 0))
        def _():
            w_own(side).start()

    @pl.loop(g + 1, G)
    def _(to):
        for i, ref, land in parts:
            kv_copy(i, ref, land, g, to).start()

    @pl.when(k == 0)
    def _():
        for i, ref, land in parts:
            kv_sib(i, ref, land, g, 0).start()

    def project(weight):
        return jnp.dot(encv[...], weight, preferred_element_type=jnp.float32).astype(jnp.bfloat16)

    def spread(plane):
        @pl.loop(1, G)
        def _(o):
            x_copy(plane, g, (g + o) % G).start()

        s_copy(plane, g, k).start()

    enc_copy.wait()
    pool[k, block(d, g)] = project(w[k]).reshape(units_g, unit, HS)
    spread(d)

    @pl.loop(1, D)
    def _(e):
        for side in (1, 0):
            src = d - e if side else d + e

            @pl.when((src >= 0) if side else (src < D))
            def _():
                w_pass(src, side).wait_recv()

                @pl.when((d + 1 < D) if side else (d > 0))
                def _():
                    w_pass(src, side).start()

                pbuf[src] = project(wall[src]).reshape(units_g, unit, HS)
                p_copy(src, d).start()

    half = T // 2

    def own_part(h):
        rows = pl.ds(h * half, half)
        sc = lax.dot_general(q[rows, :], key[...], (((1,), (1,)), ((), ())),
                             preferred_element_type=jnp.float32) * inv_root
        r = lax.broadcasted_iota(jnp.int32, sc.shape, 0) + h * half
        c = lax.broadcasted_iota(jnp.int32, sc.shape, 1)
        sc = jnp.where(c <= r, sc, NEG)
        mx = jnp.max(sc, axis=1, keepdims=True)
        ex = jnp.where(c <= r, jnp.exp(sc - mx), 0.0)
        m_ref[rows, :] = mx
        l_ref[rows, :] = jnp.sum(ex, axis=1, keepdims=True)
        acc_ref[rows, :] = jnp.dot(ex.astype(jnp.bfloat16), val[...],
                                   preferred_element_type=jnp.float32)

    for h in range(2):
        own_part(h)

    @pl.loop(0, g)
    def _(src):
        for i, ref, land in parts:
            kv_copy(i, ref, land, src, g).wait_recv()
            kv_sib(i, land.at[src * C + k], land, src, k).start()

    @pl.loop(1, D)
    def _(e):
        for side in (1, 0):
            src = d - e if side else d + e

            @pl.when((src >= 0) if side else (src < D))
            def _():
                p_copy(d, src).wait_recv()
                spread(src)

    @pl.loop(0, g)
    def _(src):
        for i, ref, land in parts:
            kv_sib(i, ref, land, src, 1 - k).wait_recv()

    @pl.when(k == 1)
    def _():
        for i, ref, land in parts:
            kv_sib(i, ref, land, g, 0).wait_recv()

    @pl.loop(0, s)
    def _(b):
        for h in range(2):
            rows = pl.ds(h * half, half)
            sc = lax.dot_general(q[rows, :], kall[b], (((1,), (1,)), ((), ())),
                                 preferred_element_type=jnp.float32) * inv_root
            old = m_ref[rows, :]
            mx = jnp.maximum(old, jnp.max(sc, axis=1, keepdims=True))
            ex = jnp.exp(sc - mx)
            fade = jnp.exp(old - mx)
            m_ref[rows, :] = mx
            l_ref[rows, :] = l_ref[rows, :] * fade + jnp.sum(ex, axis=1, keepdims=True)
            acc_ref[rows, :] = acc_ref[rows, :] * fade + jnp.dot(
                ex.astype(jnp.bfloat16), vall[b], preferred_element_type=jnp.float32)

    att[...] = (acc_ref[...] / l_ref[...]).astype(jnp.bfloat16)

    def pass_plane(plane):
        @pl.loop(1, G)
        def _(o):
            src = (g + o) % G
            x_copy(plane, src, g).wait_recv()
            s_copy(plane, src, k).start()

    pass_plane(d)

    @pl.loop(1, D)
    def _(e):
        for side in (1, 0):
            src = d - e if side else d + e

            @pl.when((src >= 0) if side else (src < D))
            def _():
                pass_plane(src)

    @pl.loop(0, D)
    def _(plane):
        @pl.loop(0, G)
        def _(src):
            s_copy(plane, src, 1 - k).wait_recv()

    for b in range(spans):
        ck, cv = (
            jnp.concatenate([pool[kv, ids[b, n] * units_tile + u]
                             for n in range(ids.shape[1]) for u in range(units_tile)], axis=0)
            for kv in range(2)
        )
        sc = lax.dot_general(cq[b * span_len:(b + 1) * span_len, :], ck, (((1,), (1,)), ((), ())),
                             preferred_element_type=jnp.float32) * inv_root
        mx = jnp.max(sc, axis=1, keepdims=True)
        ex = jnp.exp(sc - mx)
        tot = jnp.sum(ex, axis=1, keepdims=True)
        out = jnp.dot(ex.astype(jnp.bfloat16), cv, preferred_element_type=jnp.float32) / tot
        if b == 0:
            out = jnp.where(s > 0, out, 0.0)
        crs[b * span_len:(b + 1) * span_len, :] = out.astype(jnp.bfloat16)

    for side in (0, 1):
        @pl.when((d + 1 < D) if side else (d > 0))
        def _():
            w_own(side).wait_send()

            @pl.loop(0, D)
            def _(src):
                @pl.when((src < d) if side else (src > d))
                def _():
                    w_pass(src, side).wait_send()

    @pl.loop(1, D)
    def _(o):
        p_copy((d + o) % D, d).wait_send()

    @pl.loop(0, D)
    def _(plane):
        @pl.loop(1, G)
        def _(o):
            x_copy(plane, g, (g + o) % G).wait_send()

        @pl.loop(0, G)
        def _(src):
            s_copy(plane, src, k).wait_send()

    @pl.loop(g + 1, G)
    def _(to):
        for i, ref, land in parts:
            kv_copy(i, ref, land, g, to).wait_send()

    @pl.when(k == 0)
    def _():
        for i, ref, land in parts:
            kv_sib(i, ref, land, g, 0).wait_send()

    @pl.loop(0, g)
    def _(src):
        for i, ref, land in parts:
            kv_sib(i, land.at[src * C + k], land, src, k).wait_send()


def on_device(queries, keys, values, cross_queries, encoded, cross_kv_weight, owners, tile_rows):
    S, D = lax.axis_size("seq"), lax.axis_size("dp")
    G = S // 2
    T, width = queries.shape
    pool_here, tile_len, wide = encoded.shape
    rows_here = pool_here * tile_len
    rows_g = rows_here // G
    unit = math.gcd(rows_g, tile_len)
    spans_here = owners.shape[0]
    span_len = T // spans_here
    tile_index = owners * pool_here + tile_rows
    before = lax.ppermute(tile_index[-1:], "seq", [(i, i + 1) for i in range(S - 1)])
    ids = jnp.concatenate([before, tile_index], axis=0)
    padded = jnp.pad(cross_queries, ((1, span_len - 1), (0, 0)))
    w = jnp.transpose(cross_kv_weight, (1, 0, 2))
    bf, f32 = jnp.bfloat16, jnp.float32
    vm = pl.BlockSpec(memory_space=pltpu.VMEM)
    dma = pltpu.SemaphoreType.DMA
    attended, crossed = pl.pallas_call(
        functools.partial(kernel, S, D, tile_len, 1.0 / math.sqrt(HS)),
        name="retro",
        out_shape=(jax.ShapeDtypeStruct((T, width), bf), jax.ShapeDtypeStruct(padded.shape, bf)),
        in_specs=[pl.BlockSpec(memory_space=pltpu.SMEM), vm, vm, vm, vm,
                  pl.BlockSpec(memory_space=pl.ANY), vm],
        out_specs=(vm, vm),
        scratch_shapes=[
            pltpu.VMEM((rows_g, wide), bf),
            pltpu.VMEM((D, wide, HS), bf),
            pltpu.VMEM((D, rows_g // unit, unit, HS), bf),
            pltpu.VMEM((2, D * rows_here // unit, unit, HS), bf),
            pltpu.VMEM((S, T, HS), bf),
            pltpu.VMEM((S, T, HS), bf),
            pltpu.VMEM((T, 1), f32),
            pltpu.VMEM((T, 1), f32),
            pltpu.VMEM((T, HS), f32),
            dma, dma((2, D)), dma((D,)), dma((D,)), dma((D,)),
            dma((D, G)), dma((D, G)), dma((D, G)), dma((D, G)),
            dma((2, G)), dma((2, G)), dma((2, G)), dma((2, G)),
        ],
        compiler_params=pltpu.CompilerParams(
            collective_id=0, has_side_effects=True, vmem_limit_bytes=60 * 1024 * 1024),
    )(ids, queries, keys, values, padded, encoded.reshape(rows_here, wide), w)
    return attended, crossed[1:T + 1]


def solution(mesh):
    placed = (
        P("seq", "dp"),
        P("seq", "dp"),
        P("seq", "dp"),
        P("seq", "dp"),
        P("dp", None, None),
        P(None, None, "dp"),
        P("seq", None),
        P("seq", None),
    )
    return jax.shard_map(
        on_device,
        mesh=mesh,
        in_specs=placed,
        out_specs=(P("seq", "dp"), P("seq", "dp")),
        check_vma=False,
    )
```

```python
import functools
import math

import jax
import jax.numpy as jnp
from jax import lax
from jax.experimental import pallas as pl
from jax.experimental.pallas import tpu as pltpu
from jax.sharding import PartitionSpec as P

HS = 128
NEG = -1e30
MESH = pl.DeviceIdType.MESH


def kernel(
    S, D, tile_len, inv_root,
    own_s, row_s, own_h, row_h, q, key, val, cq, enc, w,
    att, crs,
    prev_v, prev_s, cqp, crf, encv, wall, pbuf, pool, kall, vall, m_ref, l_ref, acc_ref,
    enc_sem, id_send, id_recv, id_sem, send_w, recv_w, send_p, recv_p, send_x, recv_x, send_s, recv_s,
    send_k, recv_k, send_ks, recv_ks,
):
    C = 2
    G = S // C
    s = lax.axis_index("seq")
    d = lax.axis_index("dp")
    g = s // C
    k = s % C
    sib = g * C + (1 - k)
    T = q.shape[0]
    rows_g = encv.shape[0]
    near, spans_here = own_s.shape
    spans = spans_here + 1
    span_len = T // spans_here
    pool_here = (encv.shape[0] * G) // tile_len

    enc_copy = pltpu.make_async_copy(
        enc.at[pl.ds(pl.multiple_of(g * rows_g, rows_g), rows_g)], encv, enc_sem
    )
    enc_copy.start()

    bar = pltpu.get_barrier_semaphore()

    @pl.loop(1, G)
    def _(o):
        pl.semaphore_signal(bar, 1, device_id={"seq": ((g + o) % G) * C + k}, device_id_type=MESH)

    pl.semaphore_signal(bar, 1, device_id={"seq": sib}, device_id_type=MESH)

    @pl.loop(1, D)
    def _(o):
        pl.semaphore_signal(bar, 1, device_id={"dp": (d + o) % D}, device_id_type=MESH)

    nxt = (s + 1) % S
    prv = (s + S - 1) % S

    @pl.when(k == 1)
    def _():
        pl.semaphore_signal(bar, 1, device_id={"seq": nxt}, device_id_type=MESH)

    @pl.when(k == 0)
    def _():
        pl.semaphore_signal(bar, 1, device_id={"seq": prv}, device_id_type=MESH)

    pl.semaphore_wait(bar, G - 1 + 1 + D - 1 + 1)

    def id_copy(i, ref):
        return pltpu.make_async_remote_copy(
            ref, prev_v.at[i], id_send.at[i], id_recv.at[i],
            device_id={"seq": nxt}, device_id_type=MESH)

    unit = pool.shape[2]
    units_g = rows_g // unit
    units_tile = tile_len // unit

    def block(plane, group):
        return pl.ds((plane * G + group) * units_g, units_g)

    def w_own(side):
        return pltpu.make_async_remote_copy(
            w.at[k], wall.at[d], send_w.at[side, d], recv_w.at[d],
            device_id={"dp": d + (1 if side else -1)}, device_id_type=MESH)

    def w_pass(src, side):
        return pltpu.make_async_remote_copy(
            wall.at[src], wall.at[src], send_w.at[side, src], recv_w.at[src],
            device_id={"dp": d + (1 if side else -1)}, device_id_type=MESH)

    def p_copy(to, src):
        return pltpu.make_async_remote_copy(
            pbuf.at[to], pool.at[k, block(src, g)], send_p.at[to], recv_p.at[src],
            device_id={"dp": to}, device_id_type=MESH)

    def x_copy(plane, src, to):
        return pltpu.make_async_remote_copy(
            pool.at[k, block(plane, src)], pool.at[k, block(plane, src)],
            send_x.at[plane, to], recv_x.at[plane, src],
            device_id={"seq": to * C + k}, device_id_type=MESH)

    def s_copy(plane, src, kv):
        return pltpu.make_async_remote_copy(
            pool.at[kv, block(plane, src)], pool.at[kv, block(plane, src)],
            send_s.at[plane, src], recv_s.at[plane, src],
            device_id={"seq": sib}, device_id_type=MESH)

    parts = ((0, key, kall), (1, val, vall))

    def kv_copy(i, ref, land, src, to):
        return pltpu.make_async_remote_copy(
            ref, land.at[src * C + k], send_k.at[i, to], recv_k.at[i, src],
            device_id={"seq": to * C + k}, device_id_type=MESH)

    def kv_sib(i, src_ref, land, src, kk):
        return pltpu.make_async_remote_copy(
            src_ref, land.at[src * C + kk], send_ks.at[i, src], recv_ks.at[i, src],
            device_id={"seq": sib}, device_id_type=MESH)

    for side in (0, 1):
        @pl.when((d + 1 < D) if side else (d > 0))
        def _():
            w_own(side).start()

    for i, ref in ((0, own_h), (1, row_h)):
        id_copy(i, ref).start()

    @pl.loop(g + 1, G)
    def _(to):
        for i, ref, land in parts:
            kv_copy(i, ref, land, g, to).start()

    @pl.when(k == 0)
    def _():
        for i, ref, land in parts:
            kv_sib(i, ref, land, g, 0).start()

    def project(weight):
        return jnp.dot(encv[...], weight, preferred_element_type=jnp.float32).astype(jnp.bfloat16)

    def spread(plane):
        @pl.loop(1, G)
        def _(o):
            x_copy(plane, g, (g + o) % G).start()

        s_copy(plane, g, k).start()

    enc_copy.wait()
    pool[k, block(d, g)] = project(w[k]).reshape(units_g, unit, HS)
    spread(d)

    shifted = jnp.concatenate(
        [cq[...].astype(jnp.float32), jnp.zeros((span_len, HS), jnp.float32)], axis=0)
    cqp[...] = pltpu.roll(shifted, 1, 0).astype(jnp.bfloat16)

    def own_part(h):
        rows = pl.ds(h * half, half)
        sc = lax.dot_general(q[rows, :], key[...], (((1,), (1,)), ((), ())),
                             preferred_element_type=jnp.float32) * inv_root
        r = lax.broadcasted_iota(jnp.int32, sc.shape, 0) + h * half
        c = lax.broadcasted_iota(jnp.int32, sc.shape, 1)
        sc = jnp.where(c <= r, sc, NEG)
        mx = jnp.max(sc, axis=1, keepdims=True)
        ex = jnp.where(c <= r, jnp.exp(sc - mx), 0.0)
        m_ref[rows, :] = mx
        l_ref[rows, :] = jnp.sum(ex, axis=1, keepdims=True)
        acc_ref[rows, :] = jnp.dot(ex.astype(jnp.bfloat16), val[...],
                                   preferred_element_type=jnp.float32)

    half = T // 2
    for h in range(2):
        own_part(h)

    @pl.loop(1, D + 1)
    def _(e):
        @pl.when(e < D)
        def _():
            for side in (1, 0):
                src = d - e if side else d + e

                @pl.when((src >= 0) if side else (src < D))
                def _():
                    w_pass(src, side).wait_recv()

                    @pl.when((d + 1 < D) if side else (d > 0))
                    def _():
                        w_pass(src, side).start()

            for side in (1, 0):
                src = d - e if side else d + e

                @pl.when((src >= 0) if side else (src < D))
                def _():
                    pbuf[src] = project(wall[src]).reshape(units_g, unit, HS)
                    p_copy(src, d).start()

        @pl.when(e == D - 1)
        def _():
            @pl.loop(0, g)
            def _(src):
                for i, ref, land in parts:
                    kv_copy(i, ref, land, src, g).wait_recv()
                    kv_sib(i, land.at[src * C + k], land, src, k).start()

        @pl.when(e > 1)
        def _():
            for side in (1, 0):
                src = d - (e - 1) if side else d + (e - 1)

                @pl.when((src >= 0) if side else (src < D))
                def _():
                    p_copy(d, src).wait_recv()
                    spread(src)

    @pl.loop(0, g)
    def _(src):
        for i, ref, land in parts:
            kv_sib(i, ref, land, src, 1 - k).wait_recv()

    @pl.when(k == 1)
    def _():
        for i, ref, land in parts:
            kv_sib(i, ref, land, g, 0).wait_recv()

    @pl.loop(0, s)
    def _(b):
        for h in range(2):
            rows = pl.ds(h * half, half)
            sc = lax.dot_general(q[rows, :], kall[b], (((1,), (1,)), ((), ())),
                                 preferred_element_type=jnp.float32) * inv_root
            old = m_ref[rows, :]
            mx = jnp.maximum(old, jnp.max(sc, axis=1, keepdims=True))
            ex = jnp.exp(sc - mx)
            fade = jnp.exp(old - mx)
            m_ref[rows, :] = mx
            l_ref[rows, :] = l_ref[rows, :] * fade + jnp.sum(ex, axis=1, keepdims=True)
            acc_ref[rows, :] = acc_ref[rows, :] * fade + jnp.dot(
                ex.astype(jnp.bfloat16), vall[b], preferred_element_type=jnp.float32)

    att[...] = (acc_ref[...] / l_ref[...]).astype(jnp.bfloat16)

    def pass_plane(plane):
        @pl.loop(1, G)
        def _(o):
            src = (g + o) % G
            x_copy(plane, src, g).wait_recv()
            s_copy(plane, src, k).start()

    pass_plane(d)

    @pl.loop(1, D)
    def _(e):
        for side in (1, 0):
            src = d - e if side else d + e

            @pl.when((src >= 0) if side else (src < D))
            def _():
                pass_plane(src)

    @pl.loop(0, D)
    def _(plane):
        @pl.loop(0, G)
        def _(src):
            s_copy(plane, src, 1 - k).wait_recv()

    for i, ref in ((0, own_h), (1, row_h)):
        id_copy(i, ref).wait_recv()
        pltpu.make_async_copy(prev_v.at[i], prev_s.at[i], id_sem.at[i]).start()
    for i in range(2):
        pltpu.make_async_copy(prev_v.at[i], prev_s.at[i], id_sem.at[i]).wait()
    for b in range(spans):
        tiles = []
        for n in range(near):
            if b == 0:
                tiles.append(prev_s[0, n, spans_here - 1] * pool_here + prev_s[1, n, spans_here - 1])
            else:
                tiles.append(own_s[n, b - 1] * pool_here + row_s[n, b - 1])
        ck, cv = (
            jnp.concatenate([pool[kv, tile * units_tile + u]
                             for tile in tiles for u in range(units_tile)], axis=0)
            for kv in range(2)
        )
        sc = lax.dot_general(cqp[b * span_len:(b + 1) * span_len, :], ck, (((1,), (1,)), ((), ())),
                             preferred_element_type=jnp.float32) * inv_root
        mx = jnp.max(sc, axis=1, keepdims=True)
        ex = jnp.exp(sc - mx)
        tot = jnp.sum(ex, axis=1, keepdims=True)
        out = jnp.dot(ex.astype(jnp.bfloat16), cv, preferred_element_type=jnp.float32) / tot
        if b == 0:
            out = jnp.where(s > 0, out, 0.0)
        crf[b * span_len:(b + 1) * span_len, :] = out
    back = pltpu.roll(crf[...], T + span_len - 1, 0)
    crs[...] = back[:T].astype(jnp.bfloat16)

    for i, ref in ((0, own_h), (1, row_h)):
        id_copy(i, ref).wait_send()

    for side in (0, 1):
        @pl.when((d + 1 < D) if side else (d > 0))
        def _():
            w_own(side).wait_send()

            @pl.loop(0, D)
            def _(src):
                @pl.when((src < d) if side else (src > d))
                def _():
                    w_pass(src, side).wait_send()

    @pl.loop(1, D)
    def _(o):
        p_copy((d + o) % D, d).wait_send()

    @pl.loop(0, D)
    def _(plane):
        @pl.loop(1, G)
        def _(o):
            x_copy(plane, g, (g + o) % G).wait_send()

        @pl.loop(0, G)
        def _(src):
            s_copy(plane, src, k).wait_send()

    @pl.loop(g + 1, G)
    def _(to):
        for i, ref, land in parts:
            kv_copy(i, ref, land, g, to).wait_send()

    @pl.when(k == 0)
    def _():
        for i, ref, land in parts:
            kv_sib(i, ref, land, g, 0).wait_send()

    @pl.loop(0, g)
    def _(src):
        for i, ref, land in parts:
            kv_sib(i, land.at[src * C + k], land, src, k).wait_send()


def on_device(queries, keys, values, cross_queries, encoded, cross_kv_weight, owners, tile_rows):
    S, D = lax.axis_size("seq"), lax.axis_size("dp")
    G = S // 2
    T, width = queries.shape
    pool_here, tile_len, wide = encoded.shape
    rows_here = pool_here * tile_len
    rows_g = rows_here // G
    unit = math.gcd(rows_g, tile_len)
    spans_here = owners.shape[0]
    span_len = T // spans_here
    w = jnp.transpose(cross_kv_weight, (1, 0, 2))
    own, row = owners.T, tile_rows.T
    near = own.shape[0]
    bf, f32 = jnp.bfloat16, jnp.float32
    vm = pl.BlockSpec(memory_space=pltpu.VMEM)
    dma = pltpu.SemaphoreType.DMA
    attended, crossed = pl.pallas_call(
        functools.partial(kernel, S, D, tile_len, 1.0 / math.sqrt(HS)),
        name="retro",
        out_shape=(jax.ShapeDtypeStruct((T, width), bf), jax.ShapeDtypeStruct((T, width), bf)),
        in_specs=[pl.BlockSpec(memory_space=pltpu.SMEM)] * 2
                 + [pl.BlockSpec(memory_space=pl.ANY)] * 2
                 + [vm, vm, vm, vm,
                  pl.BlockSpec(memory_space=pl.ANY), vm],
        out_specs=(vm, vm),
        scratch_shapes=[
            pltpu.VMEM((2, near, spans_here), jnp.int32),
            pltpu.SMEM((2, near, spans_here), jnp.int32),
            pltpu.VMEM((T + span_len, HS), bf),
            pltpu.VMEM((T + span_len, HS), f32),
            pltpu.VMEM((rows_g, wide), bf),
            pltpu.VMEM((D, wide, HS), bf),
            pltpu.VMEM((D, rows_g // unit, unit, HS), bf),
            pltpu.VMEM((2, D * rows_here // unit, unit, HS), bf),
            pltpu.VMEM((S, T, HS), bf),
            pltpu.VMEM((S, T, HS), bf),
            pltpu.VMEM((T, 1), f32),
            pltpu.VMEM((T, 1), f32),
            pltpu.VMEM((T, HS), f32),
            dma, dma((2,)), dma((2,)), dma((2,)), dma((2, D)), dma((D,)), dma((D,)), dma((D,)),
            dma((D, G)), dma((D, G)), dma((D, G)), dma((D, G)),
            dma((2, G)), dma((2, G)), dma((2, G)), dma((2, G)),
        ],
        compiler_params=pltpu.CompilerParams(
            collective_id=0, has_side_effects=True, vmem_limit_bytes=60 * 1024 * 1024),
    )(own, row, own, row, queries, keys, values, cross_queries, encoded.reshape(rows_here, wide), w)
    return attended, crossed


def solution(mesh):
    placed = (
        P("seq", "dp"),
        P("seq", "dp"),
        P("seq", "dp"),
        P("seq", "dp"),
        P("dp", None, None),
        P(None, None, "dp"),
        P("seq", None),
        P("seq", None),
    )
    return jax.shard_map(
        on_device,
        mesh=mesh,
        in_specs=placed,
        out_specs=(P("seq", "dp"), P("seq", "dp")),
        check_vma=False,
    )
```

```python
import functools
import math

import jax
import jax.numpy as jnp
from jax import lax
from jax.experimental import pallas as pl
from jax.experimental.pallas import tpu as pltpu
from jax.sharding import PartitionSpec as P

HS = 128
NEG = -1e30
MESH = pl.DeviceIdType.MESH


def kernel(
    S, D, tile_len, inv_root,
    own_s, row_s, own_h, row_h, q, key, val, cq, enc, w,
    att, crs,
    prev_v, prev_s, cqp, crf, encv, wall, pbuf, pool, kall, vall, m_ref, l_ref, acc_ref,
    enc_sem, id_send, id_recv, id_sem, send_w, recv_w, send_p, recv_p, send_x, send_f, recv_x, send_s, recv_s,
    send_k, recv_k, send_ks, recv_ks,
):
    C = 2
    G = S // C
    s = lax.axis_index("seq")
    d = lax.axis_index("dp")
    g = s // C
    k = s % C
    sib = g * C + (1 - k)
    T = q.shape[0]
    rows_g = encv.shape[0]
    near, spans_here = own_s.shape
    spans = spans_here + 1
    span_len = T // spans_here
    pool_here = (encv.shape[0] * G) // tile_len

    enc_copy = pltpu.make_async_copy(
        enc.at[pl.ds(pl.multiple_of(g * rows_g, rows_g), rows_g)], encv, enc_sem
    )
    enc_copy.start()

    bar = pltpu.get_barrier_semaphore()

    @pl.loop(1, G)
    def _(o):
        pl.semaphore_signal(bar, 1, device_id={"seq": ((g + o) % G) * C + k}, device_id_type=MESH)

    pl.semaphore_signal(bar, 1, device_id={"seq": sib}, device_id_type=MESH)

    @pl.loop(1, D)
    def _(o):
        pl.semaphore_signal(bar, 1, device_id={"dp": (d + o) % D}, device_id_type=MESH)

    nxt = (s + 1) % S
    prv = (s + S - 1) % S

    @pl.when(k == 1)
    def _():
        pl.semaphore_signal(bar, 1, device_id={"seq": nxt}, device_id_type=MESH)

    @pl.when(k == 0)
    def _():
        pl.semaphore_signal(bar, 1, device_id={"seq": prv}, device_id_type=MESH)

    pl.semaphore_wait(bar, G - 1 + 1 + D - 1 + 1)

    def id_copy(i, ref):
        return pltpu.make_async_remote_copy(
            ref, prev_v.at[i], id_send.at[i], id_recv.at[i],
            device_id={"seq": nxt}, device_id_type=MESH)

    unit = pool.shape[2]
    units_g = rows_g // unit
    units_tile = tile_len // unit

    def block(plane, group):
        return pl.ds((plane * G + group) * units_g, units_g)

    def w_own(side):
        return pltpu.make_async_remote_copy(
            w.at[k], wall.at[d], send_w.at[side, d], recv_w.at[d],
            device_id={"dp": d + (1 if side else -1)}, device_id_type=MESH)

    def w_pass(src, side):
        return pltpu.make_async_remote_copy(
            wall.at[src], wall.at[src], send_w.at[side, src], recv_w.at[src],
            device_id={"dp": d + (1 if side else -1)}, device_id_type=MESH)

    def p_copy(to, src):
        return pltpu.make_async_remote_copy(
            pbuf.at[to], pool.at[k, block(src, g)], send_p.at[to], recv_p.at[src],
            device_id={"dp": to}, device_id_type=MESH)

    wide_x = 2 if G % 2 == 0 else 1
    high = G // wide_x
    gy, gx = g // wide_x, g % wide_x
    has_x = wide_x == 2
    gxn = gy * wide_x + (1 - gx) if has_x else g
    half_u = units_g // 2

    def up(o):
        return ((gy + o) % high) * wide_x + gx

    def x_copy(plane, src, h, to, sem):
        part = pl.ds((plane * G + src) * units_g + h * half_u, half_u)
        return pltpu.make_async_remote_copy(
            pool.at[k, part], pool.at[k, part], sem, recv_x.at[plane, h, src],
            device_id={"seq": to * C + k}, device_id_type=MESH)

    def x_own(plane, h, to):
        return x_copy(plane, g, h, to, send_x.at[plane, h, to])

    def x_fwd0(plane, to):
        return x_copy(plane, gxn, 0, to, send_f.at[plane, 0, to])

    def x_fwd1(plane, src):
        return x_copy(plane, src, 1, gxn, send_f.at[plane, 1, src])

    def x_wait(plane, src, h):
        x_copy(plane, src, h, g, recv_x.at[plane, h, src]).wait_recv()

    def s_copy(plane, src, kv):
        return pltpu.make_async_remote_copy(
            pool.at[kv, block(plane, src)], pool.at[kv, block(plane, src)],
            send_s.at[plane, src], recv_s.at[plane, src],
            device_id={"seq": sib}, device_id_type=MESH)

    parts = ((0, key, kall), (1, val, vall))

    def kv_copy(i, ref, land, src, to):
        return pltpu.make_async_remote_copy(
            ref, land.at[src * C + k], send_k.at[i, to], recv_k.at[i, src],
            device_id={"seq": to * C + k}, device_id_type=MESH)

    def kv_sib(i, src_ref, land, src, kk):
        return pltpu.make_async_remote_copy(
            src_ref, land.at[src * C + kk], send_ks.at[i, src], recv_ks.at[i, src],
            device_id={"seq": sib}, device_id_type=MESH)

    for side in (0, 1):
        @pl.when((d + 1 < D) if side else (d > 0))
        def _():
            w_own(side).start()

    for i, ref in ((0, own_h), (1, row_h)):
        id_copy(i, ref).start()

    @pl.loop(g + 1, G)
    def _(to):
        for i, ref, land in parts:
            kv_copy(i, ref, land, g, to).start()

    @pl.when(k == 0)
    def _():
        for i, ref, land in parts:
            kv_sib(i, ref, land, g, 0).start()

    def project(weight):
        return jnp.dot(encv[...], weight, preferred_element_type=jnp.float32).astype(jnp.bfloat16)

    def spread(plane):
        if has_x:
            x_own(plane, 0, gxn).start()

        @pl.loop(1, high)
        def _(o):
            x_own(plane, 1, up(o)).start()

        if has_x:
            x_own(plane, 1, gxn).start()

        @pl.loop(1, high)
        def _(o):
            x_own(plane, 0, up(o)).start()

        s_copy(plane, g, k).start()

    def relay(plane):
        if has_x:
            x_wait(plane, gxn, 0)

        @pl.loop(1, high)
        def _(o):
            if has_x:
                x_fwd0(plane, up(o)).start()
            x_wait(plane, up(o), 1)
            if has_x:
                x_fwd1(plane, up(o)).start()

        if has_x:
            x_wait(plane, gxn, 1)
            s_copy(plane, gxn, k).start()

        @pl.loop(1, high)
        def _(o):
            x_wait(plane, up(o), 0)
            s_copy(plane, up(o), k).start()

    def finish(plane):
        @pl.loop(1, high)
        def _(o):
            if has_x:
                far = ((gy + o) % high) * wide_x + (1 - gx)
                x_wait(plane, far, 0)
                x_wait(plane, far, 1)
                s_copy(plane, far, k).start()

    def at_distance(e, what):
        @pl.when(e == 0)
        def _():
            what(d)

        @pl.when(e > 0)
        def _():
            for side in (1, 0):
                src = d - e if side else d + e

                @pl.when((src >= 0) if side else (src < D))
                def _():
                    what(src)

    enc_copy.wait()
    pool[k, block(d, g)] = project(w[k]).reshape(units_g, unit, HS)
    spread(d)

    shifted = jnp.concatenate(
        [cq[...].astype(jnp.float32), jnp.zeros((span_len, HS), jnp.float32)], axis=0)
    cqp[...] = pltpu.roll(shifted, 1, 0).astype(jnp.bfloat16)

    def own_part(h):
        rows = pl.ds(h * half, half)
        sc = lax.dot_general(q[rows, :], key[...], (((1,), (1,)), ((), ())),
                             preferred_element_type=jnp.float32) * inv_root
        r = lax.broadcasted_iota(jnp.int32, sc.shape, 0) + h * half
        c = lax.broadcasted_iota(jnp.int32, sc.shape, 1)
        sc = jnp.where(c <= r, sc, NEG)
        mx = jnp.max(sc, axis=1, keepdims=True)
        ex = jnp.where(c <= r, jnp.exp(sc - mx), 0.0)
        m_ref[rows, :] = mx
        l_ref[rows, :] = jnp.sum(ex, axis=1, keepdims=True)
        acc_ref[rows, :] = jnp.dot(ex.astype(jnp.bfloat16), val[...],
                                   preferred_element_type=jnp.float32)

    half = T // 2
    for h in range(2):
        own_part(h)

    chunks = 3

    def earlier_keys(chunk):
        @pl.when(chunk == 0)
        def _():
            @pl.loop(0, g)
            def _(src):
                for i, ref, land in parts:
                    kv_sib(i, ref, land, src, 1 - k).wait_recv()

            @pl.when(k == 1)
            def _():
                for i, ref, land in parts:
                    kv_sib(i, ref, land, g, 0).wait_recv()

        @pl.loop(chunk * s // chunks, (chunk + 1) * s // chunks)
        def _(b):
            for h in range(2):
                rows = pl.ds(h * half, half)
                sc = lax.dot_general(q[rows, :], kall[b], (((1,), (1,)), ((), ())),
                                     preferred_element_type=jnp.float32) * inv_root
                old = m_ref[rows, :]
                mx = jnp.maximum(old, jnp.max(sc, axis=1, keepdims=True))
                ex = jnp.exp(sc - mx)
                fade = jnp.exp(old - mx)
                m_ref[rows, :] = mx
                l_ref[rows, :] = l_ref[rows, :] * fade + jnp.sum(ex, axis=1, keepdims=True)
                acc_ref[rows, :] = acc_ref[rows, :] * fade + jnp.dot(
                    ex.astype(jnp.bfloat16), vall[b], preferred_element_type=jnp.float32)

    @pl.loop(1, D + 2)
    def _(e):
        @pl.when(e < D)
        def _():
            for side in (1, 0):
                src = d - e if side else d + e

                @pl.when((src >= 0) if side else (src < D))
                def _():
                    w_pass(src, side).wait_recv()

                    @pl.when((d + 1 < D) if side else (d > 0))
                    def _():
                        w_pass(src, side).start()

            for side in (1, 0):
                src = d - e if side else d + e

                @pl.when((src >= 0) if side else (src < D))
                def _():
                    pbuf[src] = project(wall[src]).reshape(units_g, unit, HS)
                    p_copy(src, d).start()

        @pl.when(e == D - 1)
        def _():
            @pl.loop(0, g)
            def _(src):
                for i, ref, land in parts:
                    kv_copy(i, ref, land, src, g).wait_recv()
                    kv_sib(i, land.at[src * C + k], land, src, k).start()

        @pl.when((e > 1) & (e <= D))
        def _():
            def arrive(src):
                p_copy(d, src).wait_recv()
                spread(src)

            at_distance(e - 1, arrive)

        @pl.when(e > 1)
        def _():
            at_distance(e - 2, relay)

        @pl.when(e >= D - 1)
        def _():
            earlier_keys(e - (D - 1))

    att[...] = (acc_ref[...] / l_ref[...]).astype(jnp.bfloat16)

    @pl.loop(0, D)
    def _(e):
        at_distance(e, finish)

    @pl.loop(0, D)
    def _(plane):
        @pl.loop(0, G)
        def _(src):
            s_copy(plane, src, 1 - k).wait_recv()

    for i, ref in ((0, own_h), (1, row_h)):
        id_copy(i, ref).wait_recv()
        pltpu.make_async_copy(prev_v.at[i], prev_s.at[i], id_sem.at[i]).start()
    for i in range(2):
        pltpu.make_async_copy(prev_v.at[i], prev_s.at[i], id_sem.at[i]).wait()
    for b in range(spans):
        tiles = []
        for n in range(near):
            if b == 0:
                tiles.append(prev_s[0, n, spans_here - 1] * pool_here + prev_s[1, n, spans_here - 1])
            else:
                tiles.append(own_s[n, b - 1] * pool_here + row_s[n, b - 1])
        ck, cv = (
            jnp.concatenate([pool[kv, tile * units_tile + u]
                             for tile in tiles for u in range(units_tile)], axis=0)
            for kv in range(2)
        )
        sc = lax.dot_general(cqp[b * span_len:(b + 1) * span_len, :], ck, (((1,), (1,)), ((), ())),
                             preferred_element_type=jnp.float32) * inv_root
        mx = jnp.max(sc, axis=1, keepdims=True)
        ex = jnp.exp(sc - mx)
        tot = jnp.sum(ex, axis=1, keepdims=True)
        out = jnp.dot(ex.astype(jnp.bfloat16), cv, preferred_element_type=jnp.float32) / tot
        if b == 0:
            out = jnp.where(s > 0, out, 0.0)
        crf[b * span_len:(b + 1) * span_len, :] = out
    back = pltpu.roll(crf[...], T + span_len - 1, 0)
    crs[...] = back[:T].astype(jnp.bfloat16)

    for i, ref in ((0, own_h), (1, row_h)):
        id_copy(i, ref).wait_send()

    for side in (0, 1):
        @pl.when((d + 1 < D) if side else (d > 0))
        def _():
            w_own(side).wait_send()

            @pl.loop(0, D)
            def _(src):
                @pl.when((src < d) if side else (src > d))
                def _():
                    w_pass(src, side).wait_send()

    @pl.loop(1, D)
    def _(o):
        p_copy((d + o) % D, d).wait_send()

    @pl.loop(0, D)
    def _(plane):
        if has_x:
            for h in (0, 1):
                x_own(plane, h, gxn).wait_send()

        @pl.loop(1, high)
        def _(o):
            for h in (0, 1):
                x_own(plane, h, up(o)).wait_send()
            if has_x:
                x_fwd0(plane, up(o)).wait_send()
                x_fwd1(plane, up(o)).wait_send()

        @pl.loop(0, G)
        def _(src):
            s_copy(plane, src, k).wait_send()

    @pl.loop(g + 1, G)
    def _(to):
        for i, ref, land in parts:
            kv_copy(i, ref, land, g, to).wait_send()

    @pl.when(k == 0)
    def _():
        for i, ref, land in parts:
            kv_sib(i, ref, land, g, 0).wait_send()

    @pl.loop(0, g)
    def _(src):
        for i, ref, land in parts:
            kv_sib(i, land.at[src * C + k], land, src, k).wait_send()


def on_device(queries, keys, values, cross_queries, encoded, cross_kv_weight, owners, tile_rows):
    S, D = lax.axis_size("seq"), lax.axis_size("dp")
    G = S // 2
    T, width = queries.shape
    pool_here, tile_len, wide = encoded.shape
    rows_here = pool_here * tile_len
    rows_g = rows_here // G
    unit = math.gcd(rows_g // 2, tile_len)
    spans_here = owners.shape[0]
    span_len = T // spans_here
    w = jnp.transpose(cross_kv_weight, (1, 0, 2))
    own, row = owners.T, tile_rows.T
    near = own.shape[0]
    bf, f32 = jnp.bfloat16, jnp.float32
    vm = pl.BlockSpec(memory_space=pltpu.VMEM)
    dma = pltpu.SemaphoreType.DMA
    attended, crossed = pl.pallas_call(
        functools.partial(kernel, S, D, tile_len, 1.0 / math.sqrt(HS)),
        name="retro",
        out_shape=(jax.ShapeDtypeStruct((T, width), bf), jax.ShapeDtypeStruct((T, width), bf)),
        in_specs=[pl.BlockSpec(memory_space=pltpu.SMEM)] * 2
                 + [pl.BlockSpec(memory_space=pl.ANY)] * 2
                 + [vm, vm, vm, vm,
                  pl.BlockSpec(memory_space=pl.ANY), vm],
        out_specs=(vm, vm),
        scratch_shapes=[
            pltpu.VMEM((2, near, spans_here), jnp.int32),
            pltpu.SMEM((2, near, spans_here), jnp.int32),
            pltpu.VMEM((T + span_len, HS), bf),
            pltpu.VMEM((T + span_len, HS), f32),
            pltpu.VMEM((rows_g, wide), bf),
            pltpu.VMEM((D, wide, HS), bf),
            pltpu.VMEM((D, rows_g // unit, unit, HS), bf),
            pltpu.VMEM((2, D * rows_here // unit, unit, HS), bf),
            pltpu.VMEM((S, T, HS), bf),
            pltpu.VMEM((S, T, HS), bf),
            pltpu.VMEM((T, 1), f32),
            pltpu.VMEM((T, 1), f32),
            pltpu.VMEM((T, HS), f32),
            dma, dma((2,)), dma((2,)), dma((2,)), dma((2, D)), dma((D,)), dma((D,)), dma((D,)),
            dma((D, 2, G)), dma((D, 2, G)), dma((D, 2, G)), dma((D, G)), dma((D, G)),
            dma((2, G)), dma((2, G)), dma((2, G)), dma((2, G)),
        ],
        compiler_params=pltpu.CompilerParams(
            collective_id=0, has_side_effects=True, vmem_limit_bytes=60 * 1024 * 1024),
    )(own, row, own, row, queries, keys, values, cross_queries, encoded.reshape(rows_here, wide), w)
    return attended, crossed


def solution(mesh):
    placed = (
        P("seq", "dp"),
        P("seq", "dp"),
        P("seq", "dp"),
        P("seq", "dp"),
        P("dp", None, None),
        P(None, None, "dp"),
        P("seq", None),
        P("seq", None),
    )
    return jax.shard_map(
        on_device,
        mesh=mesh,
        in_specs=placed,
        out_specs=(P("seq", "dp"), P("seq", "dp")),
        check_vma=False,
    )
```

```python
import functools
import math

import jax
import jax.numpy as jnp
from jax import lax
from jax.experimental import pallas as pl
from jax.experimental.pallas import tpu as pltpu
from jax.sharding import PartitionSpec as P

HS = 128
NEG = -1e30
MESH = pl.DeviceIdType.MESH


def kernel(
    S, D, tile_len, inv_root,
    own_s, row_s, own_h, row_h, q, key, val, cq, enc, w,
    att, crs,
    prev_v, prev_s, cqp, crf, encv, wall, pbuf, pool, kall, vall, m_ref, l_ref, acc_ref,
    enc_sem, id_send, id_recv, id_sem, send_w, recv_w, send_p, recv_p, send_x, send_f, recv_x, send_s, recv_s,
    send_k, recv_k, send_ks, recv_ks,
):
    C = 2
    G = S // C
    s = lax.axis_index("seq")
    d = lax.axis_index("dp")
    g = s // C
    k = s % C
    sib = g * C + (1 - k)
    T = q.shape[0]
    rows_g = encv.shape[0]
    near, spans_here = own_s.shape
    spans = spans_here + 1
    span_len = T // spans_here
    pool_here = (encv.shape[0] * G) // tile_len

    enc_copy = pltpu.make_async_copy(
        enc.at[pl.ds(pl.multiple_of(g * rows_g, rows_g), rows_g)], encv, enc_sem
    )
    enc_copy.start()

    bar = pltpu.get_barrier_semaphore()

    @pl.loop(1, G)
    def _(o):
        pl.semaphore_signal(bar, 1, device_id={"seq": ((g + o) % G) * C + k}, device_id_type=MESH)

    pl.semaphore_signal(bar, 1, device_id={"seq": sib}, device_id_type=MESH)

    @pl.loop(1, D)
    def _(o):
        pl.semaphore_signal(bar, 1, device_id={"dp": (d + o) % D}, device_id_type=MESH)

    nxt = (s + 1) % S
    prv = (s + S - 1) % S

    @pl.when(k == 1)
    def _():
        pl.semaphore_signal(bar, 1, device_id={"seq": nxt}, device_id_type=MESH)

    @pl.when(k == 0)
    def _():
        pl.semaphore_signal(bar, 1, device_id={"seq": prv}, device_id_type=MESH)

    pl.semaphore_wait(bar, G - 1 + 1 + D - 1 + 1)

    def id_copy(i, ref):
        return pltpu.make_async_remote_copy(
            ref, prev_v.at[i], id_send.at[i], id_recv.at[i],
            device_id={"seq": nxt}, device_id_type=MESH)

    unit = pool.shape[2]
    units_g = rows_g // unit
    units_tile = tile_len // unit

    def block(plane, group):
        return pl.ds((plane * G + group) * units_g, units_g)

    pieces = recv_w.shape[1]
    piece = w.shape[1] // pieces

    def w_own(side, c):
        rows = pl.ds(c * piece, piece)
        return pltpu.make_async_remote_copy(
            w.at[k, rows], wall.at[d, rows], send_w.at[side, d, c], recv_w.at[d, c],
            device_id={"dp": d + (1 if side else -1)}, device_id_type=MESH)

    def w_pass(src, side, c):
        rows = pl.ds(c * piece, piece)
        return pltpu.make_async_remote_copy(
            wall.at[src, rows], wall.at[src, rows], send_w.at[side, src, c], recv_w.at[src, c],
            device_id={"dp": d + (1 if side else -1)}, device_id_type=MESH)

    def p_copy(to, src):
        return pltpu.make_async_remote_copy(
            pbuf.at[to], pool.at[k, block(src, g)], send_p.at[to], recv_p.at[src],
            device_id={"dp": to}, device_id_type=MESH)

    wide_x = 2 if G % 2 == 0 else 1
    high = G // wide_x
    gy, gx = g // wide_x, g % wide_x
    has_x = wide_x == 2
    gxn = gy * wide_x + (1 - gx) if has_x else g
    half_u = units_g // 2

    def up(o):
        return ((gy + o) % high) * wide_x + gx

    def x_copy(plane, src, h, to, sem):
        part = pl.ds((plane * G + src) * units_g + h * half_u, half_u)
        return pltpu.make_async_remote_copy(
            pool.at[k, part], pool.at[k, part], sem, recv_x.at[plane, h, src],
            device_id={"seq": to * C + k}, device_id_type=MESH)

    def x_own(plane, h, to):
        return x_copy(plane, g, h, to, send_x.at[plane, h, to])

    def x_fwd0(plane, to):
        return x_copy(plane, gxn, 0, to, send_f.at[plane, 0, to])

    def x_fwd1(plane, src):
        return x_copy(plane, src, 1, gxn, send_f.at[plane, 1, src])

    def x_wait(plane, src, h):
        x_copy(plane, src, h, g, recv_x.at[plane, h, src]).wait_recv()

    def s_copy(plane, src, kv):
        return pltpu.make_async_remote_copy(
            pool.at[kv, block(plane, src)], pool.at[kv, block(plane, src)],
            send_s.at[plane, src], recv_s.at[plane, src],
            device_id={"seq": sib}, device_id_type=MESH)

    parts = ((0, key, kall), (1, val, vall))

    def kv_copy(i, ref, land, src, to):
        return pltpu.make_async_remote_copy(
            ref, land.at[src * C + k], send_k.at[i, to], recv_k.at[i, src],
            device_id={"seq": to * C + k}, device_id_type=MESH)

    def kv_sib(i, src_ref, land, src, kk):
        return pltpu.make_async_remote_copy(
            src_ref, land.at[src * C + kk], send_ks.at[i, src], recv_ks.at[i, src],
            device_id={"seq": sib}, device_id_type=MESH)

    for c in range(pieces):
        for side in (0, 1):
            @pl.when((d + 1 < D) if side else (d > 0))
            def _():
                w_own(side, c).start()

    for i, ref in ((0, own_h), (1, row_h)):
        id_copy(i, ref).start()

    @pl.loop(g + 1, G)
    def _(to):
        for i, ref, land in parts:
            kv_copy(i, ref, land, g, to).start()

    @pl.when(k == 0)
    def _():
        for i, ref, land in parts:
            kv_sib(i, ref, land, g, 0).start()

    def project(weight):
        return jnp.dot(encv[...], weight, preferred_element_type=jnp.float32).astype(jnp.bfloat16)

    def spread(plane):
        if has_x:
            x_own(plane, 0, gxn).start()

        @pl.loop(1, high)
        def _(o):
            x_own(plane, 1, up(o)).start()

        if has_x:
            x_own(plane, 1, gxn).start()

        @pl.loop(1, high)
        def _(o):
            x_own(plane, 0, up(o)).start()

        s_copy(plane, g, k).start()

    def relay(plane):
        if has_x:
            x_wait(plane, gxn, 0)

        @pl.loop(1, high)
        def _(o):
            if has_x:
                x_fwd0(plane, up(o)).start()
            x_wait(plane, up(o), 1)
            if has_x:
                x_fwd1(plane, up(o)).start()

        if has_x:
            x_wait(plane, gxn, 1)
            s_copy(plane, gxn, k).start()

        @pl.loop(1, high)
        def _(o):
            x_wait(plane, up(o), 0)
            s_copy(plane, up(o), k).start()

    def finish(plane):
        @pl.loop(1, high)
        def _(o):
            if has_x:
                far = ((gy + o) % high) * wide_x + (1 - gx)
                x_wait(plane, far, 0)
                x_wait(plane, far, 1)
                s_copy(plane, far, k).start()

    def at_distance(e, what):
        @pl.when(e == 0)
        def _():
            what(d)

        @pl.when(e > 0)
        def _():
            for side in (1, 0):
                src = d - e if side else d + e

                @pl.when((src >= 0) if side else (src < D))
                def _():
                    what(src)

    enc_copy.wait()
    pool[k, block(d, g)] = project(w[k]).reshape(units_g, unit, HS)
    spread(d)

    shifted = jnp.concatenate(
        [cq[...].astype(jnp.float32), jnp.zeros((span_len, HS), jnp.float32)], axis=0)
    cqp[...] = pltpu.roll(shifted, 1, 0).astype(jnp.bfloat16)

    def own_part(h):
        rows = pl.ds(h * half, half)
        sc = lax.dot_general(q[rows, :], key[...], (((1,), (1,)), ((), ())),
                             preferred_element_type=jnp.float32) * inv_root
        r = lax.broadcasted_iota(jnp.int32, sc.shape, 0) + h * half
        c = lax.broadcasted_iota(jnp.int32, sc.shape, 1)
        sc = jnp.where(c <= r, sc, NEG)
        mx = jnp.max(sc, axis=1, keepdims=True)
        ex = jnp.where(c <= r, jnp.exp(sc - mx), 0.0)
        m_ref[rows, :] = mx
        l_ref[rows, :] = jnp.sum(ex, axis=1, keepdims=True)
        acc_ref[rows, :] = jnp.dot(ex.astype(jnp.bfloat16), val[...],
                                   preferred_element_type=jnp.float32)

    half = T // 2
    for h in range(2):
        own_part(h)

    chunks = 3

    def earlier_keys(chunk):
        @pl.when(chunk == 0)
        def _():
            @pl.loop(0, g)
            def _(src):
                for i, ref, land in parts:
                    kv_sib(i, ref, land, src, 1 - k).wait_recv()

            @pl.when(k == 1)
            def _():
                for i, ref, land in parts:
                    kv_sib(i, ref, land, g, 0).wait_recv()

        @pl.loop(chunk * s // chunks, (chunk + 1) * s // chunks)
        def _(b):
            for h in range(2):
                rows = pl.ds(h * half, half)
                sc = lax.dot_general(q[rows, :], kall[b], (((1,), (1,)), ((), ())),
                                     preferred_element_type=jnp.float32) * inv_root
                old = m_ref[rows, :]
                mx = jnp.maximum(old, jnp.max(sc, axis=1, keepdims=True))
                ex = jnp.exp(sc - mx)
                fade = jnp.exp(old - mx)
                m_ref[rows, :] = mx
                l_ref[rows, :] = l_ref[rows, :] * fade + jnp.sum(ex, axis=1, keepdims=True)
                acc_ref[rows, :] = acc_ref[rows, :] * fade + jnp.dot(
                    ex.astype(jnp.bfloat16), vall[b], preferred_element_type=jnp.float32)

    @pl.loop(1, D + 2)
    def _(e):
        @pl.when(e < D)
        def _():
            for c in range(pieces):
                for side in (1, 0):
                    src = d - e if side else d + e

                    @pl.when((src >= 0) if side else (src < D))
                    def _():
                        w_pass(src, side, c).wait_recv()

                        @pl.when((d + 1 < D) if side else (d > 0))
                        def _():
                            w_pass(src, side, c).start()

            for side in (1, 0):
                src = d - e if side else d + e

                @pl.when((src >= 0) if side else (src < D))
                def _():
                    pbuf[src] = project(wall[src]).reshape(units_g, unit, HS)
                    p_copy(src, d).start()

        @pl.when(e == D - 1)
        def _():
            @pl.loop(0, g)
            def _(src):
                for i, ref, land in parts:
                    kv_copy(i, ref, land, src, g).wait_recv()
                    kv_sib(i, land.at[src * C + k], land, src, k).start()

        @pl.when((e > 1) & (e <= D))
        def _():
            def arrive(src):
                p_copy(d, src).wait_recv()
                spread(src)

            at_distance(e - 1, arrive)

        @pl.when(e > 1)
        def _():
            at_distance(e - 2, relay)

        @pl.when(e >= D - 1)
        def _():
            earlier_keys(e - (D - 1))

    att[...] = (acc_ref[...] / l_ref[...]).astype(jnp.bfloat16)

    @pl.loop(0, D)
    def _(e):
        at_distance(e, finish)

    @pl.loop(0, D)
    def _(plane):
        @pl.loop(0, G)
        def _(src):
            s_copy(plane, src, 1 - k).wait_recv()

    for i, ref in ((0, own_h), (1, row_h)):
        id_copy(i, ref).wait_recv()
        pltpu.make_async_copy(prev_v.at[i], prev_s.at[i], id_sem.at[i]).start()
    for i in range(2):
        pltpu.make_async_copy(prev_v.at[i], prev_s.at[i], id_sem.at[i]).wait()
    for b in range(spans):
        tiles = []
        for n in range(near):
            if b == 0:
                tiles.append(prev_s[0, n, spans_here - 1] * pool_here + prev_s[1, n, spans_here - 1])
            else:
                tiles.append(own_s[n, b - 1] * pool_here + row_s[n, b - 1])
        ck, cv = (
            jnp.concatenate([pool[kv, tile * units_tile + u]
                             for tile in tiles for u in range(units_tile)], axis=0)
            for kv in range(2)
        )
        sc = lax.dot_general(cqp[b * span_len:(b + 1) * span_len, :], ck, (((1,), (1,)), ((), ())),
                             preferred_element_type=jnp.float32) * inv_root
        mx = jnp.max(sc, axis=1, keepdims=True)
        ex = jnp.exp(sc - mx)
        tot = jnp.sum(ex, axis=1, keepdims=True)
        out = jnp.dot(ex.astype(jnp.bfloat16), cv, preferred_element_type=jnp.float32) / tot
        if b == 0:
            out = jnp.where(s > 0, out, 0.0)
        crf[b * span_len:(b + 1) * span_len, :] = out
    back = pltpu.roll(crf[...], T + span_len - 1, 0)
    crs[...] = back[:T].astype(jnp.bfloat16)

    for i, ref in ((0, own_h), (1, row_h)):
        id_copy(i, ref).wait_send()

    for side in (0, 1):
        @pl.when((d + 1 < D) if side else (d > 0))
        def _():
            for c in range(pieces):
                w_own(side, c).wait_send()

            @pl.loop(0, D)
            def _(src):
                @pl.when((src < d) if side else (src > d))
                def _():
                    for c in range(pieces):
                        w_pass(src, side, c).wait_send()

    @pl.loop(1, D)
    def _(o):
        p_copy((d + o) % D, d).wait_send()

    @pl.loop(0, D)
    def _(plane):
        if has_x:
            for h in (0, 1):
                x_own(plane, h, gxn).wait_send()

        @pl.loop(1, high)
        def _(o):
            for h in (0, 1):
                x_own(plane, h, up(o)).wait_send()
            if has_x:
                x_fwd0(plane, up(o)).wait_send()
                x_fwd1(plane, up(o)).wait_send()

        @pl.loop(0, G)
        def _(src):
            s_copy(plane, src, k).wait_send()

    @pl.loop(g + 1, G)
    def _(to):
        for i, ref, land in parts:
            kv_copy(i, ref, land, g, to).wait_send()

    @pl.when(k == 0)
    def _():
        for i, ref, land in parts:
            kv_sib(i, ref, land, g, 0).wait_send()

    @pl.loop(0, g)
    def _(src):
        for i, ref, land in parts:
            kv_sib(i, land.at[src * C + k], land, src, k).wait_send()


def on_device(queries, keys, values, cross_queries, encoded, cross_kv_weight, owners, tile_rows):
    S, D = lax.axis_size("seq"), lax.axis_size("dp")
    G = S // 2
    T, width = queries.shape
    pool_here, tile_len, wide = encoded.shape
    rows_here = pool_here * tile_len
    rows_g = rows_here // G
    unit = math.gcd(rows_g // 2, tile_len)
    spans_here = owners.shape[0]
    span_len = T // spans_here
    w = jnp.transpose(cross_kv_weight, (1, 0, 2))
    own, row = owners.T, tile_rows.T
    near = own.shape[0]
    pieces = 4 if wide % 64 == 0 else 1
    bf, f32 = jnp.bfloat16, jnp.float32
    vm = pl.BlockSpec(memory_space=pltpu.VMEM)
    dma = pltpu.SemaphoreType.DMA
    attended, crossed = pl.pallas_call(
        functools.partial(kernel, S, D, tile_len, 1.0 / math.sqrt(HS)),
        name="retro",
        out_shape=(jax.ShapeDtypeStruct((T, width), bf), jax.ShapeDtypeStruct((T, width), bf)),
        in_specs=[pl.BlockSpec(memory_space=pltpu.SMEM)] * 2
                 + [pl.BlockSpec(memory_space=pl.ANY)] * 2
                 + [vm, vm, vm, vm,
                  pl.BlockSpec(memory_space=pl.ANY), vm],
        out_specs=(vm, vm),
        scratch_shapes=[
            pltpu.VMEM((2, near, spans_here), jnp.int32),
            pltpu.SMEM((2, near, spans_here), jnp.int32),
            pltpu.VMEM((T + span_len, HS), bf),
            pltpu.VMEM((T + span_len, HS), f32),
            pltpu.VMEM((rows_g, wide), bf),
            pltpu.VMEM((D, wide, HS), bf),
            pltpu.VMEM((D, rows_g // unit, unit, HS), bf),
            pltpu.VMEM((2, D * rows_here // unit, unit, HS), bf),
            pltpu.VMEM((S, T, HS), bf),
            pltpu.VMEM((S, T, HS), bf),
            pltpu.VMEM((T, 1), f32),
            pltpu.VMEM((T, 1), f32),
            pltpu.VMEM((T, HS), f32),
            dma, dma((2,)), dma((2,)), dma((2,)), dma((2, D, pieces)), dma((D, pieces)), dma((D,)), dma((D,)),
            dma((D, 2, G)), dma((D, 2, G)), dma((D, 2, G)), dma((D, G)), dma((D, G)),
            dma((2, G)), dma((2, G)), dma((2, G)), dma((2, G)),
        ],
        compiler_params=pltpu.CompilerParams(
            collective_id=0, has_side_effects=True, vmem_limit_bytes=60 * 1024 * 1024),
    )(own, row, own, row, queries, keys, values, cross_queries, encoded.reshape(rows_here, wide), w)
    return attended, crossed


def solution(mesh):
    placed = (
        P("seq", "dp"),
        P("seq", "dp"),
        P("seq", "dp"),
        P("seq", "dp"),
        P("dp", None, None),
        P(None, None, "dp"),
        P("seq", None),
        P("seq", None),
    )
    return jax.shard_map(
        on_device,
        mesh=mesh,
        in_specs=placed,
        out_specs=(P("seq", "dp"), P("seq", "dp")),
        check_vma=False,
    )
```

```python
import functools
import math

import jax
import jax.numpy as jnp
from jax import lax
from jax.experimental import pallas as pl
from jax.experimental.pallas import tpu as pltpu
from jax.sharding import PartitionSpec as P

HS = 128
NEG = -1e30
MESH = pl.DeviceIdType.MESH


def kernel(
    S, D, tile_len, inv_root,
    own_s, row_s, own_h, row_h, q, key, val, cq, enc, w,
    att, crs,
    prev_v, prev_s, cqp, crf, encv, wall, pbuf, pool, kall, vall, m_ref, l_ref, acc_ref,
    enc_sem, id_send, id_recv, id_sem, send_w, recv_w, send_p, recv_p, send_x, send_f, recv_x, send_s, recv_s,
    send_k, recv_k, send_ks, recv_ks,
):
    C = 2
    G = S // C
    s = lax.axis_index("seq")
    d = lax.axis_index("dp")
    g = s // C
    k = s % C
    sib = g * C + (1 - k)
    T = q.shape[0]
    rows_g = encv.shape[0]
    near, spans_here = own_s.shape
    spans = spans_here + 1
    span_len = T // spans_here
    pool_here = (encv.shape[0] * G) // tile_len

    enc_copy = pltpu.make_async_copy(
        enc.at[pl.ds(pl.multiple_of(g * rows_g, rows_g), rows_g)], encv, enc_sem
    )
    enc_copy.start()

    bar = pltpu.get_barrier_semaphore()

    @pl.loop(1, G)
    def _(o):
        pl.semaphore_signal(bar, 1, device_id={"seq": ((g + o) % G) * C + k}, device_id_type=MESH)

    pl.semaphore_signal(bar, 1, device_id={"seq": sib}, device_id_type=MESH)

    @pl.loop(1, D)
    def _(o):
        pl.semaphore_signal(bar, 1, device_id={"dp": (d + o) % D}, device_id_type=MESH)

    nxt = (s + 1) % S
    prv = (s + S - 1) % S

    @pl.when(k == 1)
    def _():
        pl.semaphore_signal(bar, 1, device_id={"seq": nxt}, device_id_type=MESH)

    @pl.when(k == 0)
    def _():
        pl.semaphore_signal(bar, 1, device_id={"seq": prv}, device_id_type=MESH)

    pl.semaphore_wait(bar, G - 1 + 1 + D - 1 + 1)

    def id_copy(i, ref):
        return pltpu.make_async_remote_copy(
            ref, prev_v.at[i], id_send.at[i], id_recv.at[i],
            device_id={"seq": nxt}, device_id_type=MESH)

    unit = pool.shape[2]
    units_g = rows_g // unit
    units_tile = tile_len // unit

    def block(plane, group):
        return pl.ds((plane * G + group) * units_g, units_g)

    pieces = recv_w.shape[1]
    piece = w.shape[1] // pieces

    def w_own(side, c):
        rows = pl.ds(c * piece, piece)
        return pltpu.make_async_remote_copy(
            w.at[k, rows], wall.at[d, rows], send_w.at[side, d, c], recv_w.at[d, c],
            device_id={"dp": d + (1 if side else -1)}, device_id_type=MESH)

    def w_pass(src, side, c):
        rows = pl.ds(c * piece, piece)
        return pltpu.make_async_remote_copy(
            wall.at[src, rows], wall.at[src, rows], send_w.at[side, src, c], recv_w.at[src, c],
            device_id={"dp": d + (1 if side else -1)}, device_id_type=MESH)

    half_u = units_g // 2

    def p_copy(to, src, h):
        return pltpu.make_async_remote_copy(
            pbuf.at[to, pl.ds(h * half_u, half_u)],
            pool.at[k, pl.ds((src * G + g) * units_g + h * half_u, half_u)],
            send_p.at[to, h], recv_p.at[src, h],
            device_id={"dp": to}, device_id_type=MESH)

    wide_x = 2 if G % 2 == 0 else 1
    high = G // wide_x
    gy, gx = g // wide_x, g % wide_x
    has_x = wide_x == 2
    gxn = gy * wide_x + (1 - gx) if has_x else g

    def up(o):
        return ((gy + o) % high) * wide_x + gx

    def x_copy(plane, src, h, to, sem):
        part = pl.ds((plane * G + src) * units_g + h * half_u, half_u)
        return pltpu.make_async_remote_copy(
            pool.at[k, part], pool.at[k, part], sem, recv_x.at[plane, h, src],
            device_id={"seq": to * C + k}, device_id_type=MESH)

    def x_own(plane, h, to):
        return x_copy(plane, g, h, to, send_x.at[plane, h, to])

    def x_fwd0(plane, to):
        return x_copy(plane, gxn, 0, to, send_f.at[plane, 0, to])

    def x_fwd1(plane, src):
        return x_copy(plane, src, 1, gxn, send_f.at[plane, 1, src])

    def x_wait(plane, src, h):
        x_copy(plane, src, h, g, recv_x.at[plane, h, src]).wait_recv()

    def s_copy(plane, src, kv):
        return pltpu.make_async_remote_copy(
            pool.at[kv, block(plane, src)], pool.at[kv, block(plane, src)],
            send_s.at[plane, src], recv_s.at[plane, src],
            device_id={"seq": sib}, device_id_type=MESH)

    parts = ((0, key, kall), (1, val, vall))

    def kv_copy(i, ref, land, src, to):
        return pltpu.make_async_remote_copy(
            ref, land.at[src * C + k], send_k.at[i, to], recv_k.at[i, src],
            device_id={"seq": to * C + k}, device_id_type=MESH)

    def kv_sib(i, src_ref, land, src, kk):
        return pltpu.make_async_remote_copy(
            src_ref, land.at[src * C + kk], send_ks.at[i, src], recv_ks.at[i, src],
            device_id={"seq": sib}, device_id_type=MESH)

    for c in range(pieces):
        for side in (0, 1):
            @pl.when((d + 1 < D) if side else (d > 0))
            def _():
                w_own(side, c).start()

    for i, ref in ((0, own_h), (1, row_h)):
        id_copy(i, ref).start()

    @pl.loop(g + 1, G)
    def _(to):
        for i, ref, land in parts:
            kv_copy(i, ref, land, g, to).start()

    @pl.when(k == 0)
    def _():
        for i, ref, land in parts:
            kv_sib(i, ref, land, g, 0).start()

    def project(weight):
        return jnp.dot(encv[...], weight, preferred_element_type=jnp.float32).astype(jnp.bfloat16)

    def spread(plane, ready):
        for h in (0, 1):
            ready(h)
            if has_x:
                x_own(plane, h, gxn).start()

            @pl.loop(1, high)
            def _(o):
                x_own(plane, h, up(o)).start()

        s_copy(plane, g, k).start()

    def relay(plane):
        if has_x:
            x_wait(plane, gxn, 0)

        @pl.loop(1, high)
        def _(o):
            if has_x:
                x_fwd0(plane, up(o)).start()
            x_wait(plane, up(o), 1)
            if has_x:
                x_fwd1(plane, up(o)).start()

        if has_x:
            x_wait(plane, gxn, 1)
            s_copy(plane, gxn, k).start()

        @pl.loop(1, high)
        def _(o):
            x_wait(plane, up(o), 0)
            s_copy(plane, up(o), k).start()

    def finish(plane):
        @pl.loop(1, high)
        def _(o):
            if has_x:
                far = ((gy + o) % high) * wide_x + (1 - gx)
                x_wait(plane, far, 0)
                x_wait(plane, far, 1)
                s_copy(plane, far, k).start()

    def at_distance(e, what):
        @pl.when(e == 0)
        def _():
            what(d)

        @pl.when(e > 0)
        def _():
            for side in (1, 0):
                src = d - e if side else d + e

                @pl.when((src >= 0) if side else (src < D))
                def _():
                    what(src)

    enc_copy.wait()
    pool[k, block(d, g)] = project(w[k]).reshape(units_g, unit, HS)
    spread(d, lambda h: None)

    shifted = jnp.concatenate(
        [cq[...].astype(jnp.float32), jnp.zeros((span_len, HS), jnp.float32)], axis=0)
    cqp[...] = pltpu.roll(shifted, 1, 0).astype(jnp.bfloat16)

    def own_part(h):
        rows = pl.ds(h * half, half)
        sc = lax.dot_general(q[rows, :], key[...], (((1,), (1,)), ((), ())),
                             preferred_element_type=jnp.float32) * inv_root
        r = lax.broadcasted_iota(jnp.int32, sc.shape, 0) + h * half
        c = lax.broadcasted_iota(jnp.int32, sc.shape, 1)
        sc = jnp.where(c <= r, sc, NEG)
        mx = jnp.max(sc, axis=1, keepdims=True)
        ex = jnp.where(c <= r, jnp.exp(sc - mx), 0.0)
        m_ref[rows, :] = mx
        l_ref[rows, :] = jnp.sum(ex, axis=1, keepdims=True)
        acc_ref[rows, :] = jnp.dot(ex.astype(jnp.bfloat16), val[...],
                                   preferred_element_type=jnp.float32)

    half = T // 2
    for h in range(2):
        own_part(h)

    chunks = 3

    def earlier_keys(chunk):
        @pl.when(chunk == 0)
        def _():
            @pl.loop(0, g)
            def _(src):
                for i, ref, land in parts:
                    kv_sib(i, ref, land, src, 1 - k).wait_recv()

            @pl.when(k == 1)
            def _():
                for i, ref, land in parts:
                    kv_sib(i, ref, land, g, 0).wait_recv()

        @pl.loop(chunk * s // chunks, (chunk + 1) * s // chunks)
        def _(b):
            for h in range(2):
                rows = pl.ds(h * half, half)
                sc = lax.dot_general(q[rows, :], kall[b], (((1,), (1,)), ((), ())),
                                     preferred_element_type=jnp.float32) * inv_root
                old = m_ref[rows, :]
                mx = jnp.maximum(old, jnp.max(sc, axis=1, keepdims=True))
                ex = jnp.exp(sc - mx)
                fade = jnp.exp(old - mx)
                m_ref[rows, :] = mx
                l_ref[rows, :] = l_ref[rows, :] * fade + jnp.sum(ex, axis=1, keepdims=True)
                acc_ref[rows, :] = acc_ref[rows, :] * fade + jnp.dot(
                    ex.astype(jnp.bfloat16), vall[b], preferred_element_type=jnp.float32)

    @pl.loop(1, D + 2)
    def _(e):
        @pl.when(e < D)
        def _():
            for c in range(pieces):
                for side in (1, 0):
                    src = d - e if side else d + e

                    @pl.when((src >= 0) if side else (src < D))
                    def _():
                        w_pass(src, side, c).wait_recv()

                        @pl.when((d + 1 < D) if side else (d > 0))
                        def _():
                            w_pass(src, side, c).start()

            for side in (1, 0):
                src = d - e if side else d + e

                @pl.when((src >= 0) if side else (src < D))
                def _():
                    pbuf[src] = project(wall[src]).reshape(units_g, unit, HS)
                    for h in (0, 1):
                        p_copy(src, d, h).start()

        @pl.when(e == D - 1)
        def _():
            @pl.loop(0, g)
            def _(src):
                for i, ref, land in parts:
                    kv_copy(i, ref, land, src, g).wait_recv()
                    kv_sib(i, land.at[src * C + k], land, src, k).start()

        @pl.when((e > 1) & (e <= D))
        def _():
            def arrive(src):
                spread(src, lambda h: p_copy(d, src, h).wait_recv())

            at_distance(e - 1, arrive)

        @pl.when(e > 1)
        def _():
            at_distance(e - 2, relay)

        @pl.when(e >= D - 1)
        def _():
            earlier_keys(e - (D - 1))

    att[...] = (acc_ref[...] / l_ref[...]).astype(jnp.bfloat16)

    @pl.loop(0, D)
    def _(e):
        at_distance(e, finish)

    @pl.loop(0, D)
    def _(plane):
        @pl.loop(0, G)
        def _(src):
            s_copy(plane, src, 1 - k).wait_recv()

    for i, ref in ((0, own_h), (1, row_h)):
        id_copy(i, ref).wait_recv()
        pltpu.make_async_copy(prev_v.at[i], prev_s.at[i], id_sem.at[i]).start()
    for i in range(2):
        pltpu.make_async_copy(prev_v.at[i], prev_s.at[i], id_sem.at[i]).wait()
    for b in range(spans):
        tiles = []
        for n in range(near):
            if b == 0:
                tiles.append(prev_s[0, n, spans_here - 1] * pool_here + prev_s[1, n, spans_here - 1])
            else:
                tiles.append(own_s[n, b - 1] * pool_here + row_s[n, b - 1])
        ck, cv = (
            jnp.concatenate([pool[kv, tile * units_tile + u]
                             for tile in tiles for u in range(units_tile)], axis=0)
            for kv in range(2)
        )
        sc = lax.dot_general(cqp[b * span_len:(b + 1) * span_len, :], ck, (((1,), (1,)), ((), ())),
                             preferred_element_type=jnp.float32) * inv_root
        mx = jnp.max(sc, axis=1, keepdims=True)
        ex = jnp.exp(sc - mx)
        tot = jnp.sum(ex, axis=1, keepdims=True)
        out = jnp.dot(ex.astype(jnp.bfloat16), cv, preferred_element_type=jnp.float32) / tot
        if b == 0:
            out = jnp.where(s > 0, out, 0.0)
        crf[b * span_len:(b + 1) * span_len, :] = out
    back = pltpu.roll(crf[...], T + span_len - 1, 0)
    crs[...] = back[:T].astype(jnp.bfloat16)

    for i, ref in ((0, own_h), (1, row_h)):
        id_copy(i, ref).wait_send()

    for side in (0, 1):
        @pl.when((d + 1 < D) if side else (d > 0))
        def _():
            for c in range(pieces):
                w_own(side, c).wait_send()

            @pl.loop(0, D)
            def _(src):
                @pl.when((src < d) if side else (src > d))
                def _():
                    for c in range(pieces):
                        w_pass(src, side, c).wait_send()

    @pl.loop(1, D)
    def _(o):
        for h in (0, 1):
            p_copy((d + o) % D, d, h).wait_send()

    @pl.loop(0, D)
    def _(plane):
        if has_x:
            for h in (0, 1):
                x_own(plane, h, gxn).wait_send()

        @pl.loop(1, high)
        def _(o):
            for h in (0, 1):
                x_own(plane, h, up(o)).wait_send()
            if has_x:
                x_fwd0(plane, up(o)).wait_send()
                x_fwd1(plane, up(o)).wait_send()

        @pl.loop(0, G)
        def _(src):
            s_copy(plane, src, k).wait_send()

    @pl.loop(g + 1, G)
    def _(to):
        for i, ref, land in parts:
            kv_copy(i, ref, land, g, to).wait_send()

    @pl.when(k == 0)
    def _():
        for i, ref, land in parts:
            kv_sib(i, ref, land, g, 0).wait_send()

    @pl.loop(0, g)
    def _(src):
        for i, ref, land in parts:
            kv_sib(i, land.at[src * C + k], land, src, k).wait_send()


def on_device(queries, keys, values, cross_queries, encoded, cross_kv_weight, owners, tile_rows):
    S, D = lax.axis_size("seq"), lax.axis_size("dp")
    G = S // 2
    T, width = queries.shape
    pool_here, tile_len, wide = encoded.shape
    rows_here = pool_here * tile_len
    rows_g = rows_here // G
    unit = math.gcd(rows_g // 2, tile_len)
    spans_here = owners.shape[0]
    span_len = T // spans_here
    w = jnp.transpose(cross_kv_weight, (1, 0, 2))
    own, row = owners.T, tile_rows.T
    near = own.shape[0]
    pieces = 4 if wide % 64 == 0 else 1
    bf, f32 = jnp.bfloat16, jnp.float32
    vm = pl.BlockSpec(memory_space=pltpu.VMEM)
    dma = pltpu.SemaphoreType.DMA
    attended, crossed = pl.pallas_call(
        functools.partial(kernel, S, D, tile_len, 1.0 / math.sqrt(HS)),
        name="retro",
        out_shape=(jax.ShapeDtypeStruct((T, width), bf), jax.ShapeDtypeStruct((T, width), bf)),
        in_specs=[pl.BlockSpec(memory_space=pltpu.SMEM)] * 2
                 + [pl.BlockSpec(memory_space=pl.ANY)] * 2
                 + [vm, vm, vm, vm,
                  pl.BlockSpec(memory_space=pl.ANY), vm],
        out_specs=(vm, vm),
        scratch_shapes=[
            pltpu.VMEM((2, near, spans_here), jnp.int32),
            pltpu.SMEM((2, near, spans_here), jnp.int32),
            pltpu.VMEM((T + span_len, HS), bf),
            pltpu.VMEM((T + span_len, HS), f32),
            pltpu.VMEM((rows_g, wide), bf),
            pltpu.VMEM((D, wide, HS), bf),
            pltpu.VMEM((D, rows_g // unit, unit, HS), bf),
            pltpu.VMEM((2, D * rows_here // unit, unit, HS), bf),
            pltpu.VMEM((S, T, HS), bf),
            pltpu.VMEM((S, T, HS), bf),
            pltpu.VMEM((T, 1), f32),
            pltpu.VMEM((T, 1), f32),
            pltpu.VMEM((T, HS), f32),
            dma, dma((2,)), dma((2,)), dma((2,)), dma((2, D, pieces)), dma((D, pieces)), dma((D, 2)), dma((D, 2)),
            dma((D, 2, G)), dma((D, 2, G)), dma((D, 2, G)), dma((D, G)), dma((D, G)),
            dma((2, G)), dma((2, G)), dma((2, G)), dma((2, G)),
        ],
        compiler_params=pltpu.CompilerParams(
            collective_id=0, has_side_effects=True, vmem_limit_bytes=60 * 1024 * 1024),
    )(own, row, own, row, queries, keys, values, cross_queries, encoded.reshape(rows_here, wide), w)
    return attended, crossed


def solution(mesh):
    placed = (
        P("seq", "dp"),
        P("seq", "dp"),
        P("seq", "dp"),
        P("seq", "dp"),
        P("dp", None, None),
        P(None, None, "dp"),
        P("seq", None),
        P("seq", None),
    )
    return jax.shard_map(
        on_device,
        mesh=mesh,
        in_specs=placed,
        out_specs=(P("seq", "dp"), P("seq", "dp")),
        check_vma=False,
    )
```

```python
import functools
import math

import jax
import jax.numpy as jnp
from jax import lax
from jax.experimental import pallas as pl
from jax.experimental.pallas import tpu as pltpu
from jax.sharding import PartitionSpec as P

HS = 128
NEG = -1e30
MESH = pl.DeviceIdType.MESH


def kernel(
    S, D, tile_len, inv_root,
    own_s, row_s, own_h, row_h, q, key, val, cq, enc, w,
    att, crs,
    prev_v, prev_s, cqp, crf, encv, wall, pbuf, pool, kall, vall, m_ref, l_ref, acc_ref,
    enc_sem, id_send, id_recv, id_sem, send_w, recv_w, send_p, recv_p, send_x, recv_x, send_s, recv_s,
    send_k, recv_k, send_ks, recv_ks,
):
    C = 2
    G = S // C
    s = lax.axis_index("seq")
    d = lax.axis_index("dp")
    g = s // C
    k = s % C
    sib = g * C + (1 - k)
    T = q.shape[0]
    rows_g = encv.shape[0]
    near, spans_here = own_s.shape
    spans = spans_here + 1
    span_len = T // spans_here
    pool_here = (encv.shape[0] * G) // tile_len

    enc_copy = pltpu.make_async_copy(
        enc.at[pl.ds(pl.multiple_of(g * rows_g, rows_g), rows_g)], encv, enc_sem
    )
    enc_copy.start()

    bar = pltpu.get_barrier_semaphore()

    @pl.loop(1, G)
    def _(o):
        pl.semaphore_signal(bar, 1, device_id={"seq": ((g + o) % G) * C + k}, device_id_type=MESH)

    pl.semaphore_signal(bar, 1, device_id={"seq": sib}, device_id_type=MESH)

    @pl.loop(1, D)
    def _(o):
        pl.semaphore_signal(bar, 1, device_id={"dp": (d + o) % D}, device_id_type=MESH)

    nxt = (s + 1) % S
    prv = (s + S - 1) % S

    @pl.when(k == 1)
    def _():
        pl.semaphore_signal(bar, 1, device_id={"seq": nxt}, device_id_type=MESH)

    @pl.when(k == 0)
    def _():
        pl.semaphore_signal(bar, 1, device_id={"seq": prv}, device_id_type=MESH)

    pl.semaphore_wait(bar, G - 1 + 1 + D - 1 + 1)

    def id_copy(i, ref):
        return pltpu.make_async_remote_copy(
            ref, prev_v.at[i], id_send.at[i], id_recv.at[i],
            device_id={"seq": nxt}, device_id_type=MESH)

    unit = pool.shape[2]
    units_g = rows_g // unit
    units_tile = tile_len // unit

    def block(plane, group):
        return pl.ds((plane * G + group) * units_g, units_g)

    pieces = recv_w.shape[1]
    piece = w.shape[1] // pieces

    def w_own(side, c):
        rows = pl.ds(c * piece, piece)
        return pltpu.make_async_remote_copy(
            w.at[k, rows], wall.at[d, rows], send_w.at[side, d, c], recv_w.at[d, c],
            device_id={"dp": d + (1 if side else -1)}, device_id_type=MESH)

    def w_pass(src, side, c):
        rows = pl.ds(c * piece, piece)
        return pltpu.make_async_remote_copy(
            wall.at[src, rows], wall.at[src, rows], send_w.at[side, src, c], recv_w.at[src, c],
            device_id={"dp": d + (1 if side else -1)}, device_id_type=MESH)

    def p_copy(to, src):
        return pltpu.make_async_remote_copy(
            pbuf.at[to], pool.at[k, block(src, g)], send_p.at[to], recv_p.at[src],
            device_id={"dp": to}, device_id_type=MESH)

    def x_copy(plane, src, to):
        return pltpu.make_async_remote_copy(
            pool.at[k, block(plane, src)], pool.at[k, block(plane, src)],
            send_x.at[plane, to], recv_x.at[plane, src],
            device_id={"seq": to * C + k}, device_id_type=MESH)

    def s_copy(plane, src, kv):
        return pltpu.make_async_remote_copy(
            pool.at[kv, block(plane, src)], pool.at[kv, block(plane, src)],
            send_s.at[plane, src], recv_s.at[plane, src],
            device_id={"seq": sib}, device_id_type=MESH)

    parts = ((0, key, kall), (1, val, vall))

    def kv_copy(i, ref, land, src, to):
        return pltpu.make_async_remote_copy(
            ref, land.at[src * C + k], send_k.at[i, to], recv_k.at[i, src],
            device_id={"seq": to * C + k}, device_id_type=MESH)

    def kv_sib(i, src_ref, land, src, kk):
        return pltpu.make_async_remote_copy(
            src_ref, land.at[src * C + kk], send_ks.at[i, src], recv_ks.at[i, src],
            device_id={"seq": sib}, device_id_type=MESH)

    for c in range(pieces):
        for side in (0, 1):
            @pl.when((d + 1 < D) if side else (d > 0))
            def _():
                w_own(side, c).start()

    for i, ref in ((0, own_h), (1, row_h)):
        id_copy(i, ref).start()

    @pl.loop(g + 1, G)
    def _(to):
        for i, ref, land in parts:
            kv_copy(i, ref, land, g, to).start()

    @pl.when(k == 0)
    def _():
        for i, ref, land in parts:
            kv_sib(i, ref, land, g, 0).start()

    def project(weight):
        return jnp.dot(encv[...], weight, preferred_element_type=jnp.float32).astype(jnp.bfloat16)

    def spread(plane):
        @pl.loop(1, G)
        def _(o):
            x_copy(plane, g, (g + o) % G).start()

        s_copy(plane, g, k).start()

    enc_copy.wait()
    pool[k, block(d, g)] = project(w[k]).reshape(units_g, unit, HS)
    spread(d)

    shifted = jnp.concatenate(
        [cq[...].astype(jnp.float32), jnp.zeros((span_len, HS), jnp.float32)], axis=0)
    cqp[...] = pltpu.roll(shifted, 1, 0).astype(jnp.bfloat16)

    def own_part(h):
        rows = pl.ds(h * half, half)
        sc = lax.dot_general(q[rows, :], key[...], (((1,), (1,)), ((), ())),
                             preferred_element_type=jnp.float32) * inv_root
        r = lax.broadcasted_iota(jnp.int32, sc.shape, 0) + h * half
        c = lax.broadcasted_iota(jnp.int32, sc.shape, 1)
        sc = jnp.where(c <= r, sc, NEG)
        mx = jnp.max(sc, axis=1, keepdims=True)
        ex = jnp.where(c <= r, jnp.exp(sc - mx), 0.0)
        m_ref[rows, :] = mx
        l_ref[rows, :] = jnp.sum(ex, axis=1, keepdims=True)
        acc_ref[rows, :] = jnp.dot(ex.astype(jnp.bfloat16), val[...],
                                   preferred_element_type=jnp.float32)

    half = T // 2
    for h in range(2):
        own_part(h)

    @pl.loop(1, D + 1)
    def _(e):
        @pl.when(e < D)
        def _():
            for c in range(pieces):
                for side in (1, 0):
                    src = d - e if side else d + e

                    @pl.when((src >= 0) if side else (src < D))
                    def _():
                        w_pass(src, side, c).wait_recv()

                        @pl.when((d + 1 < D) if side else (d > 0))
                        def _():
                            w_pass(src, side, c).start()

            for side in (1, 0):
                src = d - e if side else d + e

                @pl.when((src >= 0) if side else (src < D))
                def _():
                    pbuf[src] = project(wall[src]).reshape(units_g, unit, HS)
                    p_copy(src, d).start()

        @pl.when(e == D - 1)
        def _():
            @pl.loop(0, g)
            def _(src):
                for i, ref, land in parts:
                    kv_copy(i, ref, land, src, g).wait_recv()
                    kv_sib(i, land.at[src * C + k], land, src, k).start()

        @pl.when(e > 1)
        def _():
            for side in (1, 0):
                src = d - (e - 1) if side else d + (e - 1)

                @pl.when((src >= 0) if side else (src < D))
                def _():
                    p_copy(d, src).wait_recv()
                    spread(src)

    @pl.loop(0, g)
    def _(src):
        for i, ref, land in parts:
            kv_sib(i, ref, land, src, 1 - k).wait_recv()

    @pl.when(k == 1)
    def _():
        for i, ref, land in parts:
            kv_sib(i, ref, land, g, 0).wait_recv()

    @pl.loop(0, s)
    def _(b):
        for h in range(2):
            rows = pl.ds(h * half, half)
            sc = lax.dot_general(q[rows, :], kall[b], (((1,), (1,)), ((), ())),
                                 preferred_element_type=jnp.float32) * inv_root
            old = m_ref[rows, :]
            mx = jnp.maximum(old, jnp.max(sc, axis=1, keepdims=True))
            ex = jnp.exp(sc - mx)
            fade = jnp.exp(old - mx)
            m_ref[rows, :] = mx
            l_ref[rows, :] = l_ref[rows, :] * fade + jnp.sum(ex, axis=1, keepdims=True)
            acc_ref[rows, :] = acc_ref[rows, :] * fade + jnp.dot(
                ex.astype(jnp.bfloat16), vall[b], preferred_element_type=jnp.float32)

    att[...] = (acc_ref[...] / l_ref[...]).astype(jnp.bfloat16)

    def pass_plane(plane):
        @pl.loop(1, G)
        def _(o):
            src = (g + o) % G
            x_copy(plane, src, g).wait_recv()
            s_copy(plane, src, k).start()

    pass_plane(d)

    @pl.loop(1, D)
    def _(e):
        for side in (1, 0):
            src = d - e if side else d + e

            @pl.when((src >= 0) if side else (src < D))
            def _():
                pass_plane(src)

    @pl.loop(0, D)
    def _(plane):
        @pl.loop(0, G)
        def _(src):
            s_copy(plane, src, 1 - k).wait_recv()

    for i, ref in ((0, own_h), (1, row_h)):
        id_copy(i, ref).wait_recv()
        pltpu.make_async_copy(prev_v.at[i], prev_s.at[i], id_sem.at[i]).start()
    for i in range(2):
        pltpu.make_async_copy(prev_v.at[i], prev_s.at[i], id_sem.at[i]).wait()
    for b in range(spans):
        tiles = []
        for n in range(near):
            if b == 0:
                tiles.append(prev_s[0, n, spans_here - 1] * pool_here + prev_s[1, n, spans_here - 1])
            else:
                tiles.append(own_s[n, b - 1] * pool_here + row_s[n, b - 1])
        ck, cv = (
            jnp.concatenate([pool[kv, tile * units_tile + u]
                             for tile in tiles for u in range(units_tile)], axis=0)
            for kv in range(2)
        )
        sc = lax.dot_general(cqp[b * span_len:(b + 1) * span_len, :], ck, (((1,), (1,)), ((), ())),
                             preferred_element_type=jnp.float32) * inv_root
        mx = jnp.max(sc, axis=1, keepdims=True)
        ex = jnp.exp(sc - mx)
        tot = jnp.sum(ex, axis=1, keepdims=True)
        out = jnp.dot(ex.astype(jnp.bfloat16), cv, preferred_element_type=jnp.float32) / tot
        if b == 0:
            out = jnp.where(s > 0, out, 0.0)
        crf[b * span_len:(b + 1) * span_len, :] = out
    back = pltpu.roll(crf[...], T + span_len - 1, 0)
    crs[...] = back[:T].astype(jnp.bfloat16)

    for i, ref in ((0, own_h), (1, row_h)):
        id_copy(i, ref).wait_send()

    for side in (0, 1):
        @pl.when((d + 1 < D) if side else (d > 0))
        def _():
            for c in range(pieces):
                w_own(side, c).wait_send()

            @pl.loop(0, D)
            def _(src):
                @pl.when((src < d) if side else (src > d))
                def _():
                    for c in range(pieces):
                        w_pass(src, side, c).wait_send()

    @pl.loop(1, D)
    def _(o):
        p_copy((d + o) % D, d).wait_send()

    @pl.loop(0, D)
    def _(plane):
        @pl.loop(1, G)
        def _(o):
            x_copy(plane, g, (g + o) % G).wait_send()

        @pl.loop(0, G)
        def _(src):
            s_copy(plane, src, k).wait_send()

    @pl.loop(g + 1, G)
    def _(to):
        for i, ref, land in parts:
            kv_copy(i, ref, land, g, to).wait_send()

    @pl.when(k == 0)
    def _():
        for i, ref, land in parts:
            kv_sib(i, ref, land, g, 0).wait_send()

    @pl.loop(0, g)
    def _(src):
        for i, ref, land in parts:
            kv_sib(i, land.at[src * C + k], land, src, k).wait_send()


def on_device(queries, keys, values, cross_queries, encoded, cross_kv_weight, owners, tile_rows):
    S, D = lax.axis_size("seq"), lax.axis_size("dp")
    G = S // 2
    T, width = queries.shape
    pool_here, tile_len, wide = encoded.shape
    rows_here = pool_here * tile_len
    rows_g = rows_here // G
    unit = math.gcd(rows_g, tile_len)
    spans_here = owners.shape[0]
    span_len = T // spans_here
    w = jnp.transpose(cross_kv_weight, (1, 0, 2))
    own, row = owners.T, tile_rows.T
    near = own.shape[0]
    pieces = 4 if wide % 64 == 0 else 1
    bf, f32 = jnp.bfloat16, jnp.float32
    vm = pl.BlockSpec(memory_space=pltpu.VMEM)
    dma = pltpu.SemaphoreType.DMA
    attended, crossed = pl.pallas_call(
        functools.partial(kernel, S, D, tile_len, 1.0 / math.sqrt(HS)),
        name="retro",
        out_shape=(jax.ShapeDtypeStruct((T, width), bf), jax.ShapeDtypeStruct((T, width), bf)),
        in_specs=[pl.BlockSpec(memory_space=pltpu.SMEM)] * 2
                 + [pl.BlockSpec(memory_space=pl.ANY)] * 2
                 + [vm, vm, vm, vm,
                  pl.BlockSpec(memory_space=pl.ANY), vm],
        out_specs=(vm, vm),
        scratch_shapes=[
            pltpu.VMEM((2, near, spans_here), jnp.int32),
            pltpu.SMEM((2, near, spans_here), jnp.int32),
            pltpu.VMEM((T + span_len, HS), bf),
            pltpu.VMEM((T + span_len, HS), f32),
            pltpu.VMEM((rows_g, wide), bf),
            pltpu.VMEM((D, wide, HS), bf),
            pltpu.VMEM((D, rows_g // unit, unit, HS), bf),
            pltpu.VMEM((2, D * rows_here // unit, unit, HS), bf),
            pltpu.VMEM((S, T, HS), bf),
            pltpu.VMEM((S, T, HS), bf),
            pltpu.VMEM((T, 1), f32),
            pltpu.VMEM((T, 1), f32),
            pltpu.VMEM((T, HS), f32),
            dma, dma((2,)), dma((2,)), dma((2,)), dma((2, D, pieces)), dma((D, pieces)), dma((D,)), dma((D,)),
            dma((D, G)), dma((D, G)), dma((D, G)), dma((D, G)),
            dma((2, G)), dma((2, G)), dma((2, G)), dma((2, G)),
        ],
        compiler_params=pltpu.CompilerParams(
            collective_id=0, has_side_effects=True, vmem_limit_bytes=60 * 1024 * 1024),
    )(own, row, own, row, queries, keys, values, cross_queries, encoded.reshape(rows_here, wide), w)
    return attended, crossed


def solution(mesh):
    placed = (
        P("seq", "dp"),
        P("seq", "dp"),
        P("seq", "dp"),
        P("seq", "dp"),
        P("dp", None, None),
        P(None, None, "dp"),
        P("seq", None),
        P("seq", None),
    )
    return jax.shard_map(
        on_device,
        mesh=mesh,
        in_specs=placed,
        out_specs=(P("seq", "dp"), P("seq", "dp")),
        check_vma=False,
    )
```
